512 devices in a mesh: ctx: 32 (over x, y, core), exp: 16 (over z).
Axes of the slice: x: 4, y: 4, z: 16, core: 2. Of those that a mesh axis runs over, the one named last changes fastest.
Arguments:
- residual: bfloat16 [4096, 2048], P('ctx', 'exp'), may hold values from -60 to 60
- ssd_input: bfloat16 [4096, 2048], P('ctx', 'exp'), may hold values from -6 to 6
- state_in: bfloat16 [4096, 128], P('ctx'), may hold values from -0.015625 to 0.015625
- state_out: bfloat16 [4096, 128], P('ctx'), may hold values from -6 to 6
- log_decay: float32 [4096, 64], P('ctx', 'exp'), may hold values from -1 to 0
- skip_gain: float32 [64], P('exp'), may hold values from 0.5 to 1.5
- norm_gain: float32 [2048], P('exp'), may hold values from 0.1 to 1.9
- route_weight: float32 [4096, 2], P('ctx'), may hold values from 0.2 to 1
- expert_ids: int32 [4096, 2], P('ctx'), may hold values from 0 to 15, all different within a row; in each aligned block of 128 rows (0 to 127, 128 to 255, ...) at most 16 rows name the same one
- weight_in: bfloat16 [16, 2048, 8192], P('exp', None, 'ctx'), may hold values from -0.125 to 0.125
- weight_down: bfloat16 [16, 8192, 2048], P('exp', 'ctx'), may hold values from -0.125 to 0.125
- out_grad: bfloat16 [4096, 2048], P('ctx', 'exp'), may hold values from -6 to 6
Outputs:
- block_out: bfloat16 [4096, 2048], P('ctx', 'exp')
- grad_residual: bfloat16 [4096, 2048], P('ctx', 'exp')
- grad_input: bfloat16 [4096, 2048], P('ctx', 'exp')
- grad_weight_in: bfloat16 [16, 2048, 8192], P('exp', None, 'ctx')
- grad_weight_down: bfloat16 [16, 8192, 2048], P('exp', 'ctx')
The draws below stay inside these ranges and needn't reach their ends.
Inputs may be any that keep to these rules, and one draw needn't show every extreme that they name: `expert_ids`: the two experts of a token differ; in each aligned block of 128 rows (the tokens of one index of ctx) every expert is named by exactly 16 rows.
All inputs are finite; a program needn't handle non-finite values.
Results may differ from the reference program's by a relative error of at most 0.015.
Values may be sent and summed in bfloat16 or wider, within the bound.
No kernel may reach another device: no remote copies, remote signals or barrier semaphores. Data moves between devices by JAX's collectives and lax.ppermute only.
A program may use at most 64 MiB of HBM per device.

```python
import math
import jax
import jax.numpy as jnp
import numpy as np
from jax import lax

D = 2048
FF = 8192
HEADS = 64
STATE = 128
TOK_CTX = 128
HEAD_DIM = 32
EXPERTS = 16
CAP = 16
TOKEN_COUNT = 4096
N_CTX = 32


def draw_residual(key, part):
    random_subkeys = jax.random.split(key, 3)
    column_place = jnp.arange(D, dtype=jnp.float32) / D
    column_scale = jnp.exp(jnp.log(3.0) * column_place[None, :] + jnp.log(3.0) * jax.random.uniform(random_subkeys[1], (1, D)))
    values = jax.random.truncated_normal(random_subkeys[0], -3.0, 3.0, (TOKEN_COUNT, D))
    row_scale = 0.1 * jnp.exp(jnp.log(10.0) * jax.random.uniform(random_subkeys[2], (TOKEN_COUNT, 1)))
    return (values * row_scale * column_scale).astype(jnp.bfloat16)


def draw_log_decay(key, part):
    random_subkeys = jax.random.split(key, 5)
    lowest = jnp.log(0.05 / TOKEN_COUNT)
    upper_rate = jnp.log(1.0 / 30.0)
    baseline_rate = jnp.exp(jax.random.uniform(random_subkeys[0], (1, HEADS), minval=lowest, maxval=upper_rate))
    block_multiplier = jnp.exp(jax.random.uniform(random_subkeys[1], (TOKEN_COUNT // TOK_CTX, 1, HEADS), minval=jnp.log(0.5), maxval=jnp.log(2.0)))
    block_multiplier = jnp.broadcast_to(block_multiplier, (TOKEN_COUNT // TOK_CTX, TOK_CTX, HEADS)).reshape(TOKEN_COUNT, HEADS)
    random_offset = jax.random.uniform(random_subkeys[2], (TOKEN_COUNT, HEADS), minval=0.5, maxval=1.5)
    location_list = jax.random.randint(random_subkeys[3], (4,), 0, TOKEN_COUNT)
    spike_events = jnp.sum((jnp.arange(TOKEN_COUNT)[:, None] == location_list[None, :]).astype(jnp.float32), axis=1)
    spike_depth = jax.random.uniform(random_subkeys[4], (TOKEN_COUNT, 1), minval=0.22, maxval=0.69)
    return -(baseline_rate * block_multiplier * random_offset + jnp.minimum(spike_events, 1.0)[:, None] * spike_depth)


def with_spikes(result, own_key, source, target, blocks, factor):
    owner, partner = [(jnp.arange(result.shape[axis_at]) // (result.shape[axis_at] // blocks)).reshape([-1 if axis == axis_at else 1 for axis in range(result.ndim)]) for axis_at in (source, target)]
    chosen = jax.random.permutation(own_key, blocks)[partner]
    strong = (owner == chosen) | (owner == (partner + blocks // 2) % blocks)
    return jnp.where(strong, factor * result, result)


def levels(key, extent, pieces, least, top_value):
    def one(dim, parts):
        steps = jax.random.uniform(jax.random.fold_in(jax.random.fold_in(key, 6), dim), (parts,), jnp.float32, least / len(pieces), top_value / len(pieces))
        return jnp.repeat(jnp.exp(steps), extent[dim] // parts).reshape((-1,) + (1,) * (len(extent) - dim - 1))

    level = one(*pieces[0])
    for cut in pieces[1:]:
        level = level * one(*cut)
    return level


def deal_out(stream_key, own, number, rows, amount, top, reach, slope):
    sequence = jax.random.permutation(stream_key, amount)
    crowded, common = shares(amount, rows * top, reach, slope, True), shares(amount, rows * top, reach, slope, False)
    places = jnp.arange(amount)

    def named(lengths, turn):
        used = int((lengths > 0).sum())
        fixed = max(1, used // 4)
        shifted = fixed + (places - fixed + turn * (used - fixed)) % max(1, amount - fixed)
        return jnp.zeros((amount,), jnp.int32).at[sequence[jnp.where(places < fixed, places, shifted)]].set(jnp.asarray(lengths, jnp.int32))

    lengths = jnp.where(number % 4 == 0, named(crowded, number // 4), named(common, number - number // 4 - 1))
    mixed = jax.random.permutation(jax.random.fold_in(own, 3), amount)
    giver, receiver = mixed[0:amount // 2 * 2:2], mixed[1:amount // 2 * 2:2]
    room = jnp.minimum(lengths[giver] - 1, reach - lengths[receiver]) // 2
    room = jnp.where((giver == sequence[0]) | (receiver == sequence[0]) | (lengths[receiver] == 0), 0, jnp.maximum(room, 0))
    shifted = jax.random.randint(jax.random.fold_in(own, 4), (amount // 2,), 0, 1 << 20) % (room + 1)
    lengths = lengths.at[giver].add(-shifted).at[receiver].add(shifted)
    members = jnp.searchsorted(jnp.cumsum(lengths), jnp.arange(rows * top), side="right").astype(jnp.int32)
    listing = members.reshape(top, rows).T
    listing = listing[jax.random.permutation(jax.random.fold_in(own, 1), rows)]
    turn = jax.random.randint(jax.random.fold_in(own, 2), (rows, 1), 0, top)
    return jnp.take_along_axis(listing, (jnp.arange(top)[None, :] + turn) % top, axis=1)


def shares(number_of, total, most, lean, full):
    portions = [(1 << 20) // math.isqrt(grade ** lean) + 1 for grade in range(1, number_of + 1)]
    largest = most if full else min(most, max(-(-total // number_of), total * portions[0] // sum(portions)))
    least = 1 if total - largest >= number_of - 1 else 0
    holding, surplus = [largest] + [least] * (number_of - 1), total - largest - least * (number_of - 1)
    while surplus > 0:
        free = [i for i in range(1, number_of) if holding[i] < largest] or [i for i in range(1, number_of) if holding[i] < most]
        whole, remaining = sum([portions[i] for i in free]), surplus
        for i in free:
            addition = min(most - holding[i], max(1, remaining * portions[i] // whole), surplus)
            holding[i] = holding[i] + addition
            surplus = surplus - addition
    return np.array(holding)


def gaussian(own_key, shape, width, limit, pieces=(), kind=jnp.bfloat16):
    gain = levels(own_key, shape, pieces, -0.22, 0.18) if pieces else 1.0
    array = jax.random.normal(own_key, shape, jnp.float32) * width * gain
    return jnp.minimum(jnp.maximum(array, -limit), limit).astype(kind)


def gaussian_with(stream_key, dims, spread, bound, pieces, heavy, kind=jnp.bfloat16):
    values = spread * jax.random.normal(stream_key, dims, jnp.float32)
    if pieces:
        values = values * levels(stream_key, dims, pieces, -0.22, 0.18)
    return jnp.clip(with_spikes(values, jax.random.fold_in(stream_key, 3), *heavy), -bound, bound).astype(kind)


def setup_inputs(seed: int = 0) -> dict:
    seeds = jax.random.split(jax.random.key(seed), 13)
    residual = draw_residual(jax.random.fold_in(seeds[12], 71), 0)
    ssd_input = gaussian(seeds[1], (TOKEN_COUNT, D), 1.0, 6.0, ((0, 32), (1, 16)))
    state_in = gaussian(seeds[2], (TOKEN_COUNT, STATE), (STATE * TOKEN_COUNT // 4) ** -0.5, 0.015625, ((0, 32),))
    state_out = gaussian(seeds[3], (TOKEN_COUNT, STATE), 1.0, 6.0, ((0, 32),))
    log_decay = draw_log_decay(jax.random.fold_in(seeds[12], 71), 0)
    skip_gain = jnp.clip(0.5 + 1.0 * jax.random.uniform(seeds[5], (HEADS,), jnp.float32) ** levels(seeds[5], (HEADS,), ((0, 16),), -0.2, 0.2), 0.5, 1.5)
    norm_gain = jnp.clip(1.0 + 0.18 * jax.random.normal(seeds[6], (D,), jnp.float32), 0.1, 1.9)
    route_weight = jnp.clip(0.2 + 0.8 * jax.random.uniform(seeds[7], (TOKEN_COUNT, 2), jnp.float32) ** levels(seeds[7], (TOKEN_COUNT, 2), ((0, 32),), -0.2, 0.2), 0.2, 1.0)
    expert_ids_keys = jax.random.split(jax.random.fold_in(seeds[8], 1), TOKEN_COUNT // TOK_CTX)
    expert_ids_turns = jax.random.permutation(jax.random.fold_in(seeds[8], 3), TOKEN_COUNT // TOK_CTX)
    expert_ids = jax.vmap(lambda own, number: deal_out(jax.random.fold_in(seeds[8], 2), own, number, TOK_CTX, EXPERTS, 2, CAP, 0))(expert_ids_keys, expert_ids_turns).reshape((TOKEN_COUNT, 2))
    weight_in = gaussian(seeds[9], (EXPERTS, D, FF), D ** -0.5, 0.125, ((0, 16), (2, 32)))
    weight_down = gaussian_with(seeds[10], (EXPERTS, FF, D), FF ** -0.5, 0.125, ((0, 16), (1, 32)), (1, 2, 32, 2.75))
    out_grad = gaussian(seeds[11], (TOKEN_COUNT, D), 1.0, 6.0, ((0, 32), (1, 16)))
    return dict(residual=residual, ssd_input=ssd_input, state_in=state_in, state_out=state_out, log_decay=log_decay, skip_gain=skip_gain, norm_gain=norm_gain, route_weight=route_weight, expert_ids=expert_ids, weight_in=weight_in, weight_down=weight_down, out_grad=out_grad)


epsilon = 1e-05
highest = lax.Precision.HIGHEST

def mixing(decay_head, inner_state):
    running = jnp.cumsum(decay_head)
    gap_log = running[:, None] - running[None, :]
    location_list = jnp.arange(running.shape[0], dtype=jnp.int32)
    causal = location_list[:, None] >= location_list[None, :]
    return inner_state * jnp.exp(jnp.where(causal, gap_log, -jnp.inf))

def shard_sum(left, right):
    row_count = left.shape[0]
    shard_units = left.shape[1] // N_CTX
    left_shards = left.reshape(row_count, N_CTX, shard_units).transpose(1, 0, 2)
    right_shards = right.reshape(N_CTX, shard_units, right.shape[1])

    def accumulate(running, operands):
        product = jnp.dot(operands[0], operands[1], preferred_element_type=jnp.float32)
        rounded = lax.optimization_barrier(product.astype(jnp.bfloat16))
        return (running + rounded.astype(jnp.float32), None)
    running, unused = lax.scan(accumulate, jnp.zeros((row_count, right.shape[1]), jnp.float32), (left_shards, right_shards))
    return running.astype(jnp.bfloat16)

def expert_pass(operands):
    expert_rows, cot_rows, w_in_full, w_down_full = operands
    hidden = jnp.dot(expert_rows, w_in_full, preferred_element_type=jnp.float32)
    activated = jax.nn.silu(hidden).astype(jnp.bfloat16)
    out_rows = shard_sum(activated, w_down_full)
    d_act = jnp.dot(cot_rows, w_down_full.T, preferred_element_type=jnp.float32)
    sigmoid_h = jax.nn.sigmoid(hidden)
    d_hidden = (d_act * sigmoid_h * (1.0 + hidden * (1.0 - sigmoid_h))).astype(jnp.bfloat16)
    grad_down = jnp.dot(activated.T, cot_rows, preferred_element_type=jnp.float32).astype(jnp.bfloat16)
    grad_in = jnp.dot(expert_rows.T, d_hidden, preferred_element_type=jnp.float32).astype(jnp.bfloat16)
    d_rows = shard_sum(d_hidden, w_in_full.T)
    return (out_rows, d_rows, grad_in, grad_down)

def reference(residual, ssd_input, state_in, state_out, log_decay, skip_gain, norm_gain, route_weight, expert_ids, weight_in, weight_down, out_grad):
    inner_state = jnp.dot(state_out.astype(jnp.float32), state_in.astype(jnp.float32).T, precision=highest)
    head_input = ssd_input.astype(jnp.float32).reshape(TOKEN_COUNT, HEADS, HEAD_DIM).transpose(1, 0, 2)

    def forward_head(operands):
        return jnp.dot(mixing(operands[0], inner_state), operands[1], precision=highest)
    ssd_out = lax.map(forward_head, (log_decay.T, head_input)) + skip_gain[:, None, None] * head_input
    ssd_out = ssd_out.transpose(1, 0, 2).reshape(TOKEN_COUNT, D)
    mixed = (residual.astype(jnp.float32) + ssd_out).astype(jnp.bfloat16)
    mixed_wide = mixed.astype(jnp.float32)
    inv_rms = lax.rsqrt(lax.optimization_barrier(jnp.mean(mixed_wide * mixed_wide, axis=1, keepdims=True)) + epsilon)
    normed = (mixed_wide * inv_rms * norm_gain[None, :]).astype(jnp.bfloat16)
    route_ids = expert_ids.reshape(N_CTX, 2 * TOK_CTX)
    onehot = (route_ids[:, :, None] == jnp.arange(EXPERTS, dtype=jnp.int32)[None, None, :]).astype(jnp.int32)
    before = jnp.cumsum(onehot, axis=1) - onehot
    slot_index = lax.optimization_barrier(jnp.sum(before * onehot, axis=2))
    buffer_row = (jnp.arange(N_CTX, dtype=jnp.int32)[:, None] * CAP + slot_index).reshape(-1).astype(jnp.int32)
    expert = expert_ids.reshape(-1).astype(jnp.int32)
    route_rows = jnp.repeat(normed, 2, axis=0)
    route_cot = (route_weight.reshape(-1)[:, None] * jnp.repeat(out_grad.astype(jnp.float32), 2, axis=0)).astype(jnp.bfloat16)
    expert_rows = jnp.zeros((EXPERTS, N_CTX * CAP, D), jnp.bfloat16).at[expert, buffer_row].set(route_rows)
    cot_rows = jnp.zeros((EXPERTS, N_CTX * CAP, D), jnp.bfloat16).at[expert, buffer_row].set(route_cot)
    out_rows, d_rows, grad_in, grad_down = lax.map(expert_pass, (expert_rows, cot_rows, weight_in, weight_down))
    returned = out_rows[expert, buffer_row].astype(jnp.float32).reshape(TOKEN_COUNT, 2, D)
    expert_mix = lax.optimization_barrier(jnp.sum(returned * route_weight[:, :, None], axis=1))
    block_out = (mixed_wide + expert_mix).astype(jnp.bfloat16)
    d_normed = lax.optimization_barrier(jnp.sum(d_rows[expert, buffer_row].astype(jnp.float32).reshape(TOKEN_COUNT, 2, D), axis=1))
    scaled = norm_gain[None, :] * d_normed
    dot_terms = lax.optimization_barrier(jnp.sum(scaled * mixed_wide, axis=1, keepdims=True))
    d_mixed = out_grad.astype(jnp.float32) + inv_rms * scaled - mixed_wide * inv_rms * inv_rms * inv_rms * dot_terms / D
    head_grad = d_mixed.reshape(TOKEN_COUNT, HEADS, HEAD_DIM).transpose(1, 0, 2)

    def backward_head(operands):
        return jnp.dot(mixing(operands[0], inner_state).T, operands[1], precision=highest)
    grad_heads = lax.map(backward_head, (log_decay.T, head_grad)) + skip_gain[:, None, None] * head_grad
    grad_input = grad_heads.transpose(1, 0, 2).reshape(TOKEN_COUNT, D).astype(jnp.bfloat16)
    return (block_out, d_mixed.astype(jnp.bfloat16), grad_input, grad_in, grad_down)
```

```python
import functools
import jax
import jax.numpy as jnp
from jax import lax
from jax.experimental import pallas as pl
from jax.experimental.pallas import tpu as pltpu
from jax.sharding import PartitionSpec as P

D = 2048
epsilon = 1e-05
f32 = jnp.float32
bf16 = jnp.bfloat16


def iota(shape, axis):
    return lax.broadcasted_iota(jnp.int32, shape, axis)


def mm(a, b):
    return jnp.dot(a, b, preferred_element_type=f32)


def mm_t(a, b):
    return lax.dot_general(a, b, (((0,), (0,)), ((), ())), preferred_element_type=f32)


def mm_nt(a, b):
    return lax.dot_general(a, b, (((1,), (1,)), ((), ())), preferred_element_type=f32)


def split2(a):
    high = a.astype(bf16)
    return high, (a - high.astype(f32)).astype(bf16)


def split3(a):
    high = a.astype(bf16)
    rest = a - high.astype(f32)
    middle = rest.astype(bf16)
    return high, middle, (rest - middle.astype(f32)).astype(bf16)


def join3(parts):
    return parts[0].astype(f32) + parts[1].astype(f32) + parts[2].astype(f32)


def per_head(columns, shape, width):
    lane = iota(shape, 1)
    value = jnp.broadcast_to(columns[:, 0:1], shape)
    for head in range(1, columns.shape[1]):
        value = jnp.where(lane >= head * width, columns[:, head : head + 1], value)
    return value


def ones_where(condition, dtype=bf16):
    return jnp.where(condition, 1.0, 0.0).astype(dtype)


def call(kernel, outs, *args, smem=()):
    return pl.pallas_call(
        kernel,
        out_shape=outs,
        in_specs=[
            pl.BlockSpec(memory_space=pltpu.SMEM if i in smem else pltpu.VMEM)
            for i in range(len(args))
        ],
        out_specs=jax.tree.map(lambda o: pl.BlockSpec(memory_space=pltpu.VMEM), outs),
    )(*args)


def shape_of(shape, dtype):
    return jax.ShapeDtypeStruct(shape, dtype)


def route_kernel(ids_ref, ids_t_ref, weight_ref, grad_ref, gain_ref, to_rows_ref, from_ref, pay_ref):
    tokens, features = grad_ref.shape
    experts, _, _ = pay_ref.shape
    rows = to_rows_ref.shape[0]
    capacity = rows // experts
    square = (tokens, tokens)
    grad = grad_ref[...].astype(f32)
    hits_t = [ids_t_ref[k : k + 1, :] == iota(square, 0) for k in range(2)]
    sum_t = ones_where(hits_t[0] | hits_t[1])
    before_t = mm(sum_t, ones_where(iota(square, 0) < iota(square, 1)))
    hits = [ids_ref[:, k : k + 1] == iota(square, 1) for k in range(2)]
    both = ones_where(hits[0] | hits[1])
    before = mm(ones_where(iota(square, 1) < iota(square, 0)), both)
    spread = []
    cot = jnp.zeros((rows, features), f32)
    for k in range(2):
        slot_t = jnp.sum(jnp.where(hits_t[k], before_t, 0.0), axis=0, keepdims=True)
        row_t = ids_t_ref[k : k + 1, :] * capacity + slot_t.astype(jnp.int32)
        table_t = ones_where(iota((rows, tokens), 0) == row_t)
        spread.append(table_t)
        scaled = (weight_ref[:, k : k + 1] * grad).astype(bf16)
        cot = cot + mm(table_t, scaled)
        slot = jnp.sum(jnp.where(hits[k], before, 0.0), axis=1, keepdims=True)
        row = ids_ref[:, k : k + 1] * capacity + slot.astype(jnp.int32)
        from_ref[k] = ones_where(iota((tokens, rows), 1) == row)
    to_rows_ref[...] = spread[0] + spread[1]
    pay_ref[:, :capacity, :] = cot.astype(bf16).reshape(experts, capacity, features)
    high, middle, low = split3(gain_ref[...])
    place = iota((capacity, features), 0)
    pieces = jnp.where(
        place == 0,
        high.astype(f32),
        jnp.where(place == 1, middle.astype(f32), jnp.where(place == 2, low.astype(f32), 0.0)),
    ).astype(bf16)
    pay_ref[:, capacity:, :] = jnp.broadcast_to(pieces[None], (experts, capacity, features))


def state_kernel(x_ref, b_ref, decay_ref, pay_ref, cum_ref):
    tokens, features = x_ref.shape
    width = features // decay_ref.shape[1]
    square = (tokens, tokens)
    spread = per_head(decay_ref[...], (tokens, features), width)
    causal = ones_where(iota(square, 1) <= iota(square, 0))
    high, middle, low = split3(spread)
    cum = mm(causal, high) + mm(causal, middle) + mm(causal, low)
    cum_ref[...] = cum
    ending = cum[tokens - 1 : tokens, :]
    tail = jnp.exp(ending - cum)
    moved_high, moved_low = split2(tail * x_ref[...].astype(f32))
    b = b_ref[...]
    state = (mm_t(b, moved_high) + mm_t(b, moved_low)).astype(bf16)
    states = state.shape[0]
    parts = split3(ending)
    place = iota((pay_ref.shape[1] - states, features), 0)
    extra = jnp.where(
        place == 0,
        parts[0].astype(f32),
        jnp.where(place == 1, parts[1].astype(f32), jnp.where(place == 2, parts[2].astype(f32), 0.0)),
    ).astype(bf16)
    for j in range(pay_ref.shape[0]):
        pay_ref[j, :states, :] = state
        pay_ref[j, states:, :] = extra


def local_kernel(x_ref, b_ref, c_ref, cum_ref, skip_ref, residual_ref, local_ref, back_ref):
    tokens, features = x_ref.shape
    heads = back_ref.shape[1]
    width = features // heads
    square = (tokens, tokens)
    x = x_ref[...]
    cum = cum_ref[...]
    cum_t = cum.T
    inner = mm_nt(c_ref[...], b_ref[...])
    inner_t = mm_nt(b_ref[...], c_ref[...])
    causal = iota(square, 1) <= iota(square, 0)
    causal_t = iota(square, 0) <= iota(square, 1)
    lane = iota((tokens, features), 1)
    skip = per_head(skip_ref[...], (1, features), width)
    total = residual_ref[...].astype(f32) + skip * x.astype(f32)
    for head in range(heads):
        column = cum[:, head * width : head * width + 1]
        row = cum_t[head * width : head * width + 1, :]
        gap = jnp.where(causal, column - row, -jnp.inf)
        high, low = split2(inner * jnp.exp(gap))
        product = mm(high, x) + mm(low, x)
        inside = (lane >= head * width) & (lane < (head + 1) * width)
        total = total + jnp.where(inside, product, 0.0)
        gap_t = jnp.where(causal_t, row - column, -jnp.inf)
        high, low = split2(inner_t * jnp.exp(gap_t))
        back_ref[0, head] = high
        back_ref[1, head] = low
    local_ref[...] = total


def block_sums(states_ref, rows_at):
    blocks = states_ref.shape[0]
    features = states_ref.shape[2]
    extra = states_ref[:, rows_at : rows_at + 16, :].astype(f32)
    place = iota((blocks, 16, features), 1)
    return [
        jnp.sum(jnp.where(place == k, extra, 0.0), axis=1).astype(bf16) for k in range(3)
    ]


def weighted(states_ref, weights, states):
    total = jnp.zeros((states, states_ref.shape[2]), f32)
    for j in range(states_ref.shape[0]):
        total = total + weights[j : j + 1, :] * states_ref[j, :states, :].astype(f32)
    return total


def mixed_kernel(me_ref, states_ref, c_ref, cum_ref, local_ref, table_ref, mixed_ref, rows_ref, later_ref):
    blocks = states_ref.shape[0]
    states = c_ref.shape[1]
    me = me_ref[0]
    parts = block_sums(states_ref, states)
    source, between = iota((blocks, blocks), 0), iota((blocks, blocks), 1)
    mask = ones_where((between > source) & (between < me))
    sums = mm(mask, parts[0]) + mm(mask, parts[1]) + mm(mask, parts[2])
    which = iota((blocks, states_ref.shape[2]), 0)
    weights = jnp.where(which < me, jnp.exp(sums), 0.0)
    high, low = split2(weighted(states_ref, weights, states))
    c = c_ref[...]
    total = local_ref[...] + jnp.exp(cum_ref[...]) * (mm(c, high) + mm(c, low))
    mixed = total.astype(bf16)
    mixed_ref[...] = mixed
    rows_ref[...] = mm(table_ref[...], mixed).astype(bf16).reshape(rows_ref.shape)
    mask = ones_where((between < source) & (between > me))
    sums = mm(mask, parts[0]) + mm(mask, parts[1]) + mm(mask, parts[2])
    later_ref[...] = jnp.where(which > me, jnp.exp(sums), 0.0)


def cot_kernel(in_ref, out_ref, gain_ref):
    peers, capacity, features = in_ref.shape[0], out_ref.shape[1], in_ref.shape[2]
    for e in range(peers):
        here = slice(e * features, (e + 1) * features)
        piece = in_ref[e, :capacity, :]
        for j in range(out_ref.shape[0]):
            out_ref[j, :, here] = piece
        extra = in_ref[e, capacity : 2 * capacity, :].astype(f32)
        gain_ref[:, here] = jnp.sum(extra, axis=0, keepdims=True)


def norm_kernel(in_ref, gain_ref, out_ref, raw_ref, inv_ref):
    peers, capacity, features = in_ref.shape
    square = jnp.zeros((capacity, features), f32)
    for e in range(peers):
        piece = in_ref[e].astype(f32)
        square = square + piece * piece
    inv = lax.rsqrt(jnp.sum(square, axis=1, keepdims=True) / D + epsilon)
    inv_ref[...] = jnp.broadcast_to(inv, inv_ref.shape)
    for e in range(peers):
        here = slice(e * features, (e + 1) * features)
        piece = in_ref[e]
        raw_ref[:, here] = piece
        normed = (piece.astype(f32) * inv * gain_ref[:, here]).astype(bf16)
        for j in range(out_ref.shape[0]):
            out_ref[j, :, here] = normed


def grad_rows_kernel(parts_ref, raw_ref, inv_ref, gain_ref, out_ref):
    peers, capacity, features = out_ref.shape
    total = parts_ref[0].astype(f32)
    for j in range(1, parts_ref.shape[0]):
        total = total + parts_ref[j].astype(f32)
    total = total.astype(bf16).astype(f32)
    scaled = gain_ref[...] * total
    raw = raw_ref[...].astype(f32)
    inv = inv_ref[:, 0:1]
    inner = jnp.sum(scaled * raw, axis=1, keepdims=True)
    result = inv * scaled - raw * (inv * inv * inv * inner / D)
    for e in range(peers):
        out_ref[e] = result[:, e * features : (e + 1) * features].astype(bf16)


def out_rows_kernel(parts_ref, out_ref):
    peers, capacity, features = out_ref.shape
    total = parts_ref[0].astype(f32)
    for j in range(1, parts_ref.shape[0]):
        total = total + parts_ref[j].astype(f32)
    for e in range(peers):
        out_ref[e] = total[:, e * features : (e + 1) * features].astype(bf16)


def block_out_kernel(rows_ref, from_ref, weight_ref, mixed_ref, out_ref):
    rows = rows_ref[...].reshape(from_ref.shape[2], rows_ref.shape[2])
    total = mixed_ref[...].astype(f32)
    extra = weight_ref[:, 0:1] * mm(from_ref[0], rows) + weight_ref[:, 1:2] * mm(from_ref[1], rows)
    out_ref[...] = (total + extra).astype(bf16)


def cot_state_kernel(rows_ref, from_ref, grad_ref, c_ref, cum_ref, residual_ref, wide_ref, pay_ref):
    rows = rows_ref[...].reshape(from_ref.shape[2], rows_ref.shape[2])
    table = from_ref[0] + from_ref[1]
    total = grad_ref[...].astype(f32) + mm(table, rows)
    wide_ref[...] = total
    residual_ref[...] = total.astype(bf16)
    high, low = split2(jnp.exp(cum_ref[...]) * total)
    c = c_ref[...]
    state = (mm_t(c, high) + mm_t(c, low)).astype(bf16)
    for j in range(pay_ref.shape[0]):
        pay_ref[j] = state


def back_local_kernel(wide_ref, back_ref, skip_ref, out_ref):
    tokens, features = wide_ref.shape
    heads = back_ref.shape[1]
    width = features // heads
    wide = wide_ref[...]
    high, low = split2(wide)
    lane = iota((tokens, features), 1)
    total = per_head(skip_ref[...], (1, features), width) * wide
    for head in range(heads):
        product = mm(back_ref[0, head], high) + mm(back_ref[1, head], high) + mm(back_ref[0, head], low)
        inside = (lane >= head * width) & (lane < (head + 1) * width)
        total = total + jnp.where(inside, product, 0.0)
    out_ref[...] = total


def final_kernel(states_ref, later_ref, b_ref, cum_ref, local_ref, out_ref):
    tokens = cum_ref.shape[0]
    high, low = split2(weighted(states_ref, later_ref[...], states_ref.shape[1]))
    cum = cum_ref[...]
    tail = jnp.exp(cum[tokens - 1 : tokens, :] - cum)
    b = b_ref[...]
    out_ref[...] = (local_ref[...] + tail * (mm(b, high) + mm(b, low))).astype(bf16)


def swap(a, axis):
    return lax.all_to_all(a, axis, split_axis=0, concat_axis=0, tiled=True)


def body(
    residual,
    ssd_input,
    state_in,
    state_out,
    log_decay,
    skip_gain,
    norm_gain,
    route_weight,
    expert_ids,
    weight_in,
    weight_down,
    out_grad,
):
    tokens, features = residual.shape
    heads = log_decay.shape[1]
    states = state_in.shape[1]
    experts = lax.axis_size("exp")
    blocks = lax.axis_size("ctx")
    rows = 2 * tokens
    capacity = rows // experts
    me = lax.axis_index("ctx").astype(jnp.int32).reshape(1)
    skip = skip_gain.reshape(1, heads)
    matrix_in = weight_in[0]
    matrix_down = weight_down[0]

    state_pay, cum = call(
        state_kernel,
        (shape_of((blocks, states + 16, features), bf16), shape_of((tokens, features), f32)),
        ssd_input, state_in, log_decay,
    )
    state_all = swap(state_pay, "ctx")

    to_rows, from_rows, cot_pay = call(
        route_kernel,
        (
            shape_of((rows, tokens), bf16),
            shape_of((2, tokens, rows), bf16),
            shape_of((experts, 2 * capacity, features), bf16),
        ),
        expert_ids, expert_ids.T, route_weight, out_grad, norm_gain.reshape(1, features),
    )
    cot_arrived = swap(cot_pay, "exp")
    local, back = call(
        local_kernel,
        (shape_of((tokens, features), f32), shape_of((2, heads, tokens, tokens), bf16)),
        ssd_input, state_in, state_out, cum, skip, residual,
    )
    cot_spread, gain = call(
        cot_kernel,
        (shape_of((blocks, capacity, D), bf16), shape_of((1, D), f32)),
        cot_arrived,
    )
    cot_rows = swap(cot_spread, "ctx").reshape(blocks * capacity, D)
    d_act = mm_nt(cot_rows, matrix_down)

    mixed, mixed_rows, later = call(
        mixed_kernel,
        (
            shape_of((tokens, features), bf16),
            shape_of((experts, capacity, features), bf16),
            shape_of((blocks, features), f32),
        ),
        me, state_all, state_out, cum, local, to_rows,
        smem=(0,),
    )
    arrived = swap(mixed_rows, "exp")
    normed_spread, raw, inv = call(
        norm_kernel,
        (
            shape_of((blocks, capacity, D), bf16),
            shape_of((capacity, D), bf16),
            shape_of((capacity, 128), f32),
        ),
        arrived, gain,
    )
    expert_rows = swap(normed_spread, "ctx").reshape(blocks * capacity, D)

    hidden = mm(expert_rows, matrix_in)
    sigmoid_h = jax.nn.sigmoid(hidden)
    d_hidden = (d_act * sigmoid_h * (1.0 + hidden * (1.0 - sigmoid_h))).astype(bf16)
    d_parts = mm_nt(d_hidden, matrix_in).astype(bf16).reshape(blocks, capacity, D)
    d_all = swap(d_parts, "ctx")
    activated = (hidden * sigmoid_h).astype(bf16)
    out_parts = mm(activated, matrix_down).astype(bf16).reshape(blocks, capacity, D)
    out_all = swap(out_parts, "ctx")
    grad_down = mm_t(activated, cot_rows).astype(bf16)
    grad_in = mm_t(expert_rows, d_hidden).astype(bf16)

    d_back = call(
        grad_rows_kernel, shape_of((experts, capacity, features), bf16), d_all, raw, inv, gain
    )
    d_returned = swap(d_back, "exp")
    out_back = call(out_rows_kernel, shape_of((experts, capacity, features), bf16), out_all)
    out_returned = swap(out_back, "exp")

    grad_residual, wide, cot_pay_state = call(
        cot_state_kernel,
        (
            shape_of((tokens, features), bf16),
            shape_of((tokens, features), f32),
            shape_of((blocks, states, features), bf16),
        ),
        d_returned, from_rows, out_grad, state_out, cum,
    )
    cot_states = swap(cot_pay_state, "ctx")
    back_local = call(
        back_local_kernel, shape_of((tokens, features), f32), wide, back, skip
    )
    block_out = call(
        block_out_kernel, shape_of((tokens, features), bf16), out_returned, from_rows, route_weight, mixed
    )
    grad_input = call(
        final_kernel, shape_of((tokens, features), bf16), cot_states, later, state_in, cum, back_local
    )
    return (block_out, grad_residual, grad_input, grad_in[None], grad_down[None])


def solution(mesh):
    placed = (
        P("ctx", "exp"),
        P("ctx", "exp"),
        P("ctx", None),
        P("ctx", None),
        P("ctx", "exp"),
        P("exp"),
        P("exp"),
        P("ctx", None),
        P("ctx", None),
        P("exp", None, "ctx"),
        P("exp", "ctx", None),
        P("ctx", "exp"),
    )
    return jax.shard_map(
        body,
        mesh=mesh,
        in_specs=placed,
        out_specs=(
            P("ctx", "exp"),
            P("ctx", "exp"),
            P("ctx", "exp"),
            P("exp", None, "ctx"),
            P("exp", "ctx", None),
        ),
        check_vma=False,
    )
```

```python
import functools
import jax
import jax.numpy as jnp
from jax import lax
from jax.experimental import pallas as pl
from jax.experimental.pallas import tpu as pltpu
from jax.sharding import PartitionSpec as P

D = 2048
epsilon = 1e-05
f32 = jnp.float32
bf16 = jnp.bfloat16


def iota(shape, axis):
    return lax.broadcasted_iota(jnp.int32, shape, axis)


def mm(a, b):
    return jnp.dot(a, b, preferred_element_type=f32)


def mm_t(a, b):
    return lax.dot_general(a, b, (((0,), (0,)), ((), ())), preferred_element_type=f32)


def mm_nt(a, b):
    return lax.dot_general(a, b, (((1,), (1,)), ((), ())), preferred_element_type=f32)


def split2(a):
    high = a.astype(bf16)
    return high, (a - high.astype(f32)).astype(bf16)


def split3(a):
    high = a.astype(bf16)
    rest = a - high.astype(f32)
    middle = rest.astype(bf16)
    return high, middle, (rest - middle.astype(f32)).astype(bf16)


def join3(parts):
    return parts[0].astype(f32) + parts[1].astype(f32) + parts[2].astype(f32)


def per_head(columns, shape, width):
    lane = iota(shape, 1)
    value = jnp.broadcast_to(columns[:, 0:1], shape)
    for head in range(1, columns.shape[1]):
        value = jnp.where(lane >= head * width, columns[:, head : head + 1], value)
    return value


def ones_where(condition, dtype=bf16):
    return jnp.where(condition, 1.0, 0.0).astype(dtype)


def call(kernel, outs, *args, smem=()):
    return pl.pallas_call(
        kernel,
        out_shape=outs,
        in_specs=[
            pl.BlockSpec(memory_space=pltpu.SMEM if i in smem else pltpu.VMEM)
            for i in range(len(args))
        ],
        out_specs=jax.tree.map(lambda o: pl.BlockSpec(memory_space=pltpu.VMEM), outs),
    )(*args)


def shape_of(shape, dtype):
    return jax.ShapeDtypeStruct(shape, dtype)


def route_kernel(ids_ref, ids_t_ref, weight_ref, grad_ref, gain_ref, to_rows_ref, from_ref, pay_ref):
    tokens, features = grad_ref.shape
    experts, _, _ = pay_ref.shape
    rows = to_rows_ref.shape[0]
    capacity = rows // experts
    square = (tokens, tokens)
    grad = grad_ref[...].astype(f32)
    hits_t = [ids_t_ref[k : k + 1, :] == iota(square, 0) for k in range(2)]
    sum_t = ones_where(hits_t[0] | hits_t[1])
    before_t = mm(sum_t, ones_where(iota(square, 0) < iota(square, 1)))
    hits = [ids_ref[:, k : k + 1] == iota(square, 1) for k in range(2)]
    both = ones_where(hits[0] | hits[1])
    before = mm(ones_where(iota(square, 1) < iota(square, 0)), both)
    spread = []
    cot = jnp.zeros((rows, features), f32)
    for k in range(2):
        slot_t = jnp.sum(jnp.where(hits_t[k], before_t, 0.0), axis=0, keepdims=True)
        row_t = ids_t_ref[k : k + 1, :] * capacity + slot_t.astype(jnp.int32)
        table_t = ones_where(iota((rows, tokens), 0) == row_t)
        spread.append(table_t)
        scaled = (weight_ref[:, k : k + 1] * grad).astype(bf16)
        cot = cot + mm(table_t, scaled)
        slot = jnp.sum(jnp.where(hits[k], before, 0.0), axis=1, keepdims=True)
        row = ids_ref[:, k : k + 1] * capacity + slot.astype(jnp.int32)
        from_ref[k] = ones_where(iota((tokens, rows), 1) == row)
    to_rows_ref[...] = spread[0] + spread[1]
    pay_ref[:, :capacity, :] = cot.astype(bf16).reshape(experts, capacity, features)
    high, middle, low = split3(gain_ref[...])
    place = iota((capacity, features), 0)
    pieces = jnp.where(
        place == 0,
        high.astype(f32),
        jnp.where(place == 1, middle.astype(f32), jnp.where(place == 2, low.astype(f32), 0.0)),
    ).astype(bf16)
    pay_ref[:, capacity:, :] = jnp.broadcast_to(pieces[None], (experts, capacity, features))


def state_kernel(x_ref, b_ref, decay_ref, pay_ref, cum_ref):
    tokens, features = x_ref.shape
    width = features // decay_ref.shape[1]
    square = (tokens, tokens)
    spread = per_head(decay_ref[...], (tokens, features), width)
    causal = ones_where(iota(square, 1) <= iota(square, 0))
    high, middle, low = split3(spread)
    cum = mm(causal, high) + mm(causal, middle) + mm(causal, low)
    cum_ref[...] = cum
    ending = cum[tokens - 1 : tokens, :]
    tail = jnp.exp(ending - cum)
    moved_high, moved_low = split2(tail * x_ref[...].astype(f32))
    b = b_ref[...]
    state = (mm_t(b, moved_high) + mm_t(b, moved_low)).astype(bf16)
    states = state.shape[0]
    parts = split3(ending)
    place = iota((pay_ref.shape[1] - states, features), 0)
    extra = jnp.where(
        place == 0,
        parts[0].astype(f32),
        jnp.where(place == 1, parts[1].astype(f32), jnp.where(place == 2, parts[2].astype(f32), 0.0)),
    ).astype(bf16)
    for j in range(pay_ref.shape[0]):
        pay_ref[j, :states, :] = state
        pay_ref[j, states:, :] = extra


def local_kernel(x_ref, b_ref, c_ref, cum_ref, skip_ref, residual_ref, local_ref, back_ref):
    tokens, features = x_ref.shape
    heads = back_ref.shape[1]
    width = features // heads
    square = (tokens, tokens)
    x = x_ref[...]
    cum = cum_ref[...]
    cum_t = cum.T
    inner = mm_nt(c_ref[...], b_ref[...])
    inner_t = mm_nt(b_ref[...], c_ref[...])
    causal = iota(square, 1) <= iota(square, 0)
    causal_t = iota(square, 0) <= iota(square, 1)
    lane = iota((tokens, features), 1)
    skip = per_head(skip_ref[...], (1, features), width)
    total = residual_ref[...].astype(f32) + skip * x.astype(f32)
    for head in range(heads):
        column = cum[:, head * width : head * width + 1]
        row = cum_t[head * width : head * width + 1, :]
        gap = jnp.where(causal, column - row, -jnp.inf)
        high, low = split2(inner * jnp.exp(gap))
        product = mm(high, x) + mm(low, x)
        inside = (lane >= head * width) & (lane < (head + 1) * width)
        total = total + jnp.where(inside, product, 0.0)
        gap_t = jnp.where(causal_t, row - column, -jnp.inf)
        high, low = split2(inner_t * jnp.exp(gap_t))
        back_ref[0, head] = high
        back_ref[1, head] = low
    local_ref[...] = total


def block_sums(states_ref, rows_at):
    blocks = states_ref.shape[0]
    features = states_ref.shape[2]
    extra = states_ref[:, rows_at : rows_at + 16, :].astype(f32)
    place = iota((blocks, 16, features), 1)
    return [
        jnp.sum(jnp.where(place == k, extra, 0.0), axis=1).astype(bf16) for k in range(3)
    ]


def weighted(states_ref, weights, states):
    total = jnp.zeros((states, states_ref.shape[2]), f32)
    for j in range(states_ref.shape[0]):
        total = total + weights[j : j + 1, :] * states_ref[j, :states, :].astype(f32)
    return total


def mixed_kernel(me_ref, states_ref, c_ref, cum_ref, local_ref, table_ref, early_ref, mixed_ref, pay_ref, later_ref):
    blocks = states_ref.shape[0]
    states = c_ref.shape[1]
    me = me_ref[0]
    parts = block_sums(states_ref, states)
    source, between = iota((blocks, blocks), 0), iota((blocks, blocks), 1)
    mask = ones_where((between > source) & (between < me))
    sums = mm(mask, parts[0]) + mm(mask, parts[1]) + mm(mask, parts[2])
    which = iota((blocks, states_ref.shape[2]), 0)
    weights = jnp.where(which < me, jnp.exp(sums), 0.0)
    high, low = split2(weighted(states_ref, weights, states))
    c = c_ref[...]
    total = local_ref[...] + jnp.exp(cum_ref[...]) * (mm(c, high) + mm(c, low))
    mixed = total.astype(bf16)
    mixed_ref[...] = mixed
    experts, total_rows, features = pay_ref.shape
    capacity = table_ref.shape[0] // experts
    pay_ref[:, :capacity, :] = (
        mm(table_ref[...], mixed).astype(bf16).reshape(experts, capacity, features)
    )
    pay_ref[:, capacity:, :] = early_ref[...]
    mask = ones_where((between < source) & (between > me))
    sums = mm(mask, parts[0]) + mm(mask, parts[1]) + mm(mask, parts[2])
    later_ref[...] = jnp.where(which > me, jnp.exp(sums), 0.0)


def norm_kernel(in_ref, out_ref, raw_ref, inv_ref, gain_ref):
    peers, _, features = in_ref.shape
    capacity = raw_ref.shape[0]
    square = jnp.zeros((capacity, features), f32)
    for e in range(peers):
        piece = in_ref[e, :capacity, :].astype(f32)
        square = square + piece * piece
    inv = lax.rsqrt(jnp.sum(square, axis=1, keepdims=True) / D + epsilon)
    inv_ref[...] = jnp.broadcast_to(inv, inv_ref.shape)
    for e in range(peers):
        here = slice(e * features, (e + 1) * features)
        piece = in_ref[e, :capacity, :]
        cot = in_ref[e, capacity : 2 * capacity, :]
        gain = jnp.sum(in_ref[e, 2 * capacity :, :].astype(f32), axis=0, keepdims=True)
        gain_ref[:, here] = gain
        raw_ref[:, here] = piece
        normed = (piece.astype(f32) * inv * gain).astype(bf16)
        for j in range(out_ref.shape[0]):
            out_ref[j, :capacity, here] = normed
            out_ref[j, capacity:, here] = cot


def expert_kernel(rows_ref, in_ref, in_peer_ref, down_ref, down_peer_ref, parts_ref, mine_ref, peer_ref):
    chips, both, width = rows_ref.shape
    capacity = both // 2
    count = chips * capacity
    rows = rows_ref[:, :capacity, :].reshape(count, width)
    cot = rows_ref[:, capacity:, :].reshape(count, width)
    d_total = None
    out_total = None
    for wide, narrow, kept in ((in_ref, down_ref, mine_ref), (in_peer_ref, down_peer_ref, peer_ref)):
        hidden = mm(rows, wide[...])
        d_act = mm_nt(cot, narrow[...])
        sigmoid_h = 1.0 / (1.0 + jnp.exp(-hidden))
        activated = (hidden * sigmoid_h).astype(bf16)
        d_hidden = (d_act * sigmoid_h * (1.0 + hidden * (1.0 - sigmoid_h))).astype(bf16)
        kept[0] = activated
        kept[1] = d_hidden
        d_part = mm_nt(d_hidden, wide[...])
        out_part = mm(activated, narrow[...])
        d_total = d_part if d_total is None else d_total + d_part
        out_total = out_part if out_total is None else out_total + out_part
    parts_ref[:, :capacity, :] = d_total.astype(bf16).reshape(chips, capacity, width)
    parts_ref[:, capacity:, :] = out_total.astype(bf16).reshape(chips, capacity, width)


def return_kernel(parts_ref, raw_ref, inv_ref, gain_ref, out_ref):
    peers, both, features = out_ref.shape
    capacity = both // 2
    total = parts_ref[0].astype(f32)
    for j in range(1, parts_ref.shape[0]):
        total = total + parts_ref[j].astype(f32)
    d_rows = total[:capacity].astype(bf16).astype(f32)
    out_rows = total[capacity:]
    scaled = gain_ref[...] * d_rows
    raw = raw_ref[...].astype(f32)
    inv = inv_ref[:, 0:1]
    inner = jnp.sum(scaled * raw, axis=1, keepdims=True)
    result = inv * scaled - raw * (inv * inv * inv * inner / D)
    for e in range(peers):
        here = slice(e * features, (e + 1) * features)
        out_ref[e, :capacity, :] = result[:, here].astype(bf16)
        out_ref[e, capacity:, :] = out_rows[:, here].astype(bf16)


def block_out_kernel(rows_ref, from_ref, weight_ref, mixed_ref, out_ref):
    half = rows_ref.shape[1] // 2
    rows = rows_ref[:, half:, :].reshape(from_ref.shape[2], rows_ref.shape[2])
    total = mixed_ref[...].astype(f32)
    extra = weight_ref[:, 0:1] * mm(from_ref[0], rows) + weight_ref[:, 1:2] * mm(from_ref[1], rows)
    out_ref[...] = (total + extra).astype(bf16)


def cot_state_kernel(rows_ref, from_ref, grad_ref, c_ref, cum_ref, residual_ref, wide_ref, pay_ref):
    half = rows_ref.shape[1] // 2
    rows = rows_ref[:, :half, :].reshape(from_ref.shape[2], rows_ref.shape[2])
    table = from_ref[0] + from_ref[1]
    total = grad_ref[...].astype(f32) + mm(table, rows)
    wide_ref[...] = total
    residual_ref[...] = total.astype(bf16)
    high, low = split2(jnp.exp(cum_ref[...]) * total)
    c = c_ref[...]
    state = (mm_t(c, high) + mm_t(c, low)).astype(bf16)
    for j in range(pay_ref.shape[0]):
        pay_ref[j] = state


def back_local_kernel(wide_ref, back_ref, skip_ref, out_ref):
    tokens, features = wide_ref.shape
    heads = back_ref.shape[1]
    width = features // heads
    wide = wide_ref[...]
    high, low = split2(wide)
    lane = iota((tokens, features), 1)
    total = per_head(skip_ref[...], (1, features), width) * wide
    for head in range(heads):
        product = mm(back_ref[0, head], high) + mm(back_ref[1, head], high) + mm(back_ref[0, head], low)
        inside = (lane >= head * width) & (lane < (head + 1) * width)
        total = total + jnp.where(inside, product, 0.0)
    out_ref[...] = total


def final_kernel(states_ref, later_ref, b_ref, cum_ref, local_ref, out_ref):
    tokens = cum_ref.shape[0]
    high, low = split2(weighted(states_ref, later_ref[...], states_ref.shape[1]))
    cum = cum_ref[...]
    tail = jnp.exp(cum[tokens - 1 : tokens, :] - cum)
    b = b_ref[...]
    out_ref[...] = (local_ref[...] + tail * (mm(b, high) + mm(b, low))).astype(bf16)


def swap(a, axis, groups=None):
    return lax.all_to_all(
        a, axis, split_axis=0, concat_axis=0, tiled=True, axis_index_groups=groups
    )


def body(
    residual,
    ssd_input,
    state_in,
    state_out,
    log_decay,
    skip_gain,
    norm_gain,
    route_weight,
    expert_ids,
    weight_in,
    weight_down,
    out_grad,
):
    tokens, features = residual.shape
    heads = log_decay.shape[1]
    states = state_in.shape[1]
    experts = lax.axis_size("exp")
    blocks = lax.axis_size("ctx")
    rows = 2 * tokens
    capacity = rows // experts
    me = lax.axis_index("ctx").astype(jnp.int32).reshape(1)
    skip = skip_gain.reshape(1, heads)
    matrix_in = weight_in[0]
    matrix_down = weight_down[0]

    chips = blocks // 2
    same_core = [[2 * chip + core for chip in range(chips)] for core in range(2)]
    partners = [(i, i ^ 1) for i in range(blocks)]

    def partner(a):
        return lax.ppermute(a, "ctx", partners)

    state_pay, cum = call(
        state_kernel,
        (shape_of((blocks, states + 16, features), bf16), shape_of((tokens, features), f32)),
        ssd_input, state_in, log_decay,
    )
    state_all = swap(state_pay, "ctx")
    peer_in = partner(matrix_in)
    peer_down = partner(matrix_down)

    to_rows, from_rows, cot_pay = call(
        route_kernel,
        (
            shape_of((rows, tokens), bf16),
            shape_of((2, tokens, rows), bf16),
            shape_of((experts, 2 * capacity, features), bf16),
        ),
        expert_ids, expert_ids.T, route_weight, out_grad, norm_gain.reshape(1, features),
    )
    local, back = call(
        local_kernel,
        (shape_of((tokens, features), f32), shape_of((2, heads, tokens, tokens), bf16)),
        ssd_input, state_in, state_out, cum, skip, residual,
    )
    mixed, rows_pay, later = call(
        mixed_kernel,
        (
            shape_of((tokens, features), bf16),
            shape_of((experts, 3 * capacity, features), bf16),
            shape_of((blocks, features), f32),
        ),
        me, state_all, state_out, cum, local, to_rows, cot_pay,
        smem=(0,),
    )
    arrived = swap(rows_pay, "exp")
    spread, raw, inv, gain = call(
        norm_kernel,
        (
            shape_of((chips, 2 * capacity, D), bf16),
            shape_of((capacity, D), bf16),
            shape_of((capacity, 128), f32),
            shape_of((1, D), f32),
        ),
        arrived,
    )
    expert_rows = swap(spread, "ctx", same_core)

    units = matrix_in.shape[1]
    count = chips * capacity
    parts, mine, peer = call(
        expert_kernel,
        (
            shape_of((chips, 2 * capacity, D), bf16),
            shape_of((2, count, units), bf16),
            shape_of((2, count, units), bf16),
        ),
        expert_rows, matrix_in, peer_in, matrix_down, peer_down,
    )
    parts_all = swap(parts, "ctx", same_core)
    peer_rows = partner(expert_rows)
    peer_units = partner(peer)
    all_rows = jnp.concatenate([expert_rows[:, :capacity], peer_rows[:, :capacity]]).reshape(-1, D)
    all_cot = jnp.concatenate([expert_rows[:, capacity:], peer_rows[:, capacity:]]).reshape(-1, D)
    all_units = jnp.concatenate([mine, peer_units], axis=1)
    grad_down = mm_t(all_units[0], all_cot).astype(bf16)
    grad_in = mm_t(all_rows, all_units[1]).astype(bf16)

    back_pay = call(
        return_kernel,
        shape_of((experts, 2 * capacity, features), bf16),
        parts_all, raw, inv, gain,
    )
    returned = swap(back_pay, "exp")

    grad_residual, wide, cot_pay_state = call(
        cot_state_kernel,
        (
            shape_of((tokens, features), bf16),
            shape_of((tokens, features), f32),
            shape_of((blocks, states, features), bf16),
        ),
        returned, from_rows, out_grad, state_out, cum,
    )
    cot_states = swap(cot_pay_state, "ctx")
    back_local = call(
        back_local_kernel, shape_of((tokens, features), f32), wide, back, skip
    )
    block_out = call(
        block_out_kernel, shape_of((tokens, features), bf16), returned, from_rows, route_weight, mixed
    )
    grad_input = call(
        final_kernel, shape_of((tokens, features), bf16), cot_states, later, state_in, cum, back_local
    )
    return (block_out, grad_residual, grad_input, grad_in[None], grad_down[None])


def solution(mesh):
    placed = (
        P("ctx", "exp"),
        P("ctx", "exp"),
        P("ctx", None),
        P("ctx", None),
        P("ctx", "exp"),
        P("exp"),
        P("exp"),
        P("ctx", None),
        P("ctx", None),
        P("exp", None, "ctx"),
        P("exp", "ctx", None),
        P("ctx", "exp"),
    )
    return jax.shard_map(
        body,
        mesh=mesh,
        in_specs=placed,
        out_specs=(
            P("ctx", "exp"),
            P("ctx", "exp"),
            P("ctx", "exp"),
            P("exp", None, "ctx"),
            P("exp", "ctx", None),
        ),
        check_vma=False,
    )
```

```python
import functools
import jax
import jax.numpy as jnp
from jax import lax
from jax.experimental import pallas as pl
from jax.experimental.pallas import tpu as pltpu
from jax.sharding import PartitionSpec as P

D = 2048
epsilon = 1e-05
f32 = jnp.float32
bf16 = jnp.bfloat16


def iota(shape, axis):
    return lax.broadcasted_iota(jnp.int32, shape, axis)


def mm(a, b):
    return jnp.dot(a, b, preferred_element_type=f32)


def mm_t(a, b):
    return lax.dot_general(a, b, (((0,), (0,)), ((), ())), preferred_element_type=f32)


def mm_nt(a, b):
    return lax.dot_general(a, b, (((1,), (1,)), ((), ())), preferred_element_type=f32)


def split2(a):
    high = a.astype(bf16)
    return high, (a - high.astype(f32)).astype(bf16)


def split3(a):
    high = a.astype(bf16)
    rest = a - high.astype(f32)
    middle = rest.astype(bf16)
    return high, middle, (rest - middle.astype(f32)).astype(bf16)


def join3(parts):
    return parts[0].astype(f32) + parts[1].astype(f32) + parts[2].astype(f32)


def per_head(columns, shape, width):
    lane = iota(shape, 1)
    value = jnp.broadcast_to(columns[:, 0:1], shape)
    for head in range(1, columns.shape[1]):
        value = jnp.where(lane >= head * width, columns[:, head : head + 1], value)
    return value


def ones_where(condition, dtype=bf16):
    return jnp.where(condition, 1.0, 0.0).astype(dtype)


def call(kernel, outs, *args, smem=(), near=()):
    args = [
        pltpu.with_memory_space_constraint(a, pltpu.VMEM) if a.ndim > 2 or i in near else a
        for i, a in enumerate(args)
    ]
    return pl.pallas_call(
        kernel,
        out_shape=outs,
        in_specs=[
            pl.BlockSpec(memory_space=pltpu.SMEM if i in smem else pltpu.VMEM)
            for i in range(len(args))
        ],
        out_specs=jax.tree.map(lambda o: pl.BlockSpec(memory_space=pltpu.VMEM), outs),
    )(*args)


def shape_of(shape, dtype):
    return jax.ShapeDtypeStruct(shape, dtype)


def route_kernel(ids_ref, ids_t_ref, weight_ref, grad_ref, gain_ref, to_rows_ref, from_ref, pay_ref):
    tokens, features = grad_ref.shape
    experts, _, _ = pay_ref.shape
    rows = to_rows_ref.shape[0]
    capacity = rows // experts
    square = (tokens, tokens)
    grad = grad_ref[...].astype(f32)
    hits_t = [ids_t_ref[k : k + 1, :] == iota(square, 0) for k in range(2)]
    sum_t = ones_where(hits_t[0] | hits_t[1])
    before_t = mm(sum_t, ones_where(iota(square, 0) < iota(square, 1)))
    hits = [ids_ref[:, k : k + 1] == iota(square, 1) for k in range(2)]
    both = ones_where(hits[0] | hits[1])
    before = mm(ones_where(iota(square, 1) < iota(square, 0)), both)
    spread = []
    cot = jnp.zeros((rows, features), f32)
    for k in range(2):
        slot_t = jnp.sum(jnp.where(hits_t[k], before_t, 0.0), axis=0, keepdims=True)
        row_t = ids_t_ref[k : k + 1, :] * capacity + slot_t.astype(jnp.int32)
        table_t = ones_where(iota((rows, tokens), 0) == row_t)
        spread.append(table_t)
        scaled = (weight_ref[:, k : k + 1] * grad).astype(bf16)
        cot = cot + mm(table_t, scaled)
        slot = jnp.sum(jnp.where(hits[k], before, 0.0), axis=1, keepdims=True)
        row = ids_ref[:, k : k + 1] * capacity + slot.astype(jnp.int32)
        from_ref[k] = ones_where(iota((tokens, rows), 1) == row)
    to_rows_ref[...] = spread[0] + spread[1]
    pay_ref[:, :capacity, :] = cot.astype(bf16).reshape(experts, capacity, features)
    high, middle, low = split3(gain_ref[...])
    place = iota((pay_ref.shape[1] - capacity, features), 0)
    pieces = jnp.where(
        place == 0,
        high.astype(f32),
        jnp.where(place == 1, middle.astype(f32), jnp.where(place == 2, low.astype(f32), 0.0)),
    ).astype(bf16)
    pay_ref[:, capacity:, :] = jnp.broadcast_to(pieces[None], (experts,) + pieces.shape)


def state_kernel(x_ref, b_ref, decay_ref, pay_ref, cum_ref):
    tokens, features = x_ref.shape
    heads = decay_ref.shape[0]
    width = features // heads
    square = (tokens, tokens)
    place = iota((features, tokens), 0)
    spread = jnp.broadcast_to(decay_ref[0:1, :], (features, tokens))
    for head in range(1, heads):
        spread = jnp.where(place >= head * width, decay_ref[head : head + 1, :], spread)
    causal = ones_where(iota(square, 0) <= iota(square, 1))
    high, middle, low = split3(spread)
    cum = (mm(high, causal) + mm(middle, causal) + mm(low, causal)).T
    cum_ref[...] = cum
    ending = cum[tokens - 1 : tokens, :]
    tail = jnp.exp(ending - cum)
    moved_high, moved_low = split2(tail * x_ref[...].astype(f32))
    b = b_ref[...]
    state = (mm_t(b, moved_high) + mm_t(b, moved_low)).astype(bf16)
    states = state.shape[0]
    parts = split3(ending)
    place = iota((pay_ref.shape[1] - states, features), 0)
    extra = jnp.where(
        place == 0,
        parts[0].astype(f32),
        jnp.where(place == 1, parts[1].astype(f32), jnp.where(place == 2, parts[2].astype(f32), 0.0)),
    ).astype(bf16)
    for j in range(pay_ref.shape[0]):
        pay_ref[j, :states, :] = state
        pay_ref[j, states:, :] = extra


def local_kernel(x_ref, b_ref, c_ref, cum_ref, skip_ref, residual_ref, local_ref, back_ref):
    tokens, features = x_ref.shape
    heads = back_ref.shape[1]
    width = features // heads
    square = (tokens, tokens)
    x = x_ref[...]
    cum = cum_ref[...]
    cum_t = cum.T
    inner = mm_nt(c_ref[...], b_ref[...])
    inner_t = mm_nt(b_ref[...], c_ref[...])
    causal = iota(square, 1) <= iota(square, 0)
    causal_t = iota(square, 0) <= iota(square, 1)
    lane = iota((tokens, features), 1)
    skip = per_head(skip_ref[...], (1, features), width)
    total = residual_ref[...].astype(f32) + skip * x.astype(f32)
    for head in range(heads):
        column = cum[:, head * width : head * width + 1]
        row = cum_t[head * width : head * width + 1, :]
        gap = jnp.where(causal, column - row, -jnp.inf)
        high, low = split2(inner * jnp.exp(gap))
        product = mm(high, x) + mm(low, x)
        inside = (lane >= head * width) & (lane < (head + 1) * width)
        total = total + jnp.where(inside, product, 0.0)
        gap_t = jnp.where(causal_t, row - column, -jnp.inf)
        high, low = split2(inner_t * jnp.exp(gap_t))
        back_ref[0, head] = high
        back_ref[1, head] = low
    local_ref[...] = total


def block_sums(states_ref, rows_at):
    blocks = states_ref.shape[0]
    features = states_ref.shape[2]
    extra = states_ref[:, rows_at : rows_at + 16, :].astype(f32)
    place = iota((blocks, 16, features), 1)
    return [
        jnp.sum(jnp.where(place == k, extra, 0.0), axis=1).astype(bf16) for k in range(3)
    ]


def weighted(states_ref, weights, states):
    total = jnp.zeros((states, states_ref.shape[2]), f32)
    for j in range(states_ref.shape[0]):
        total = total + weights[j : j + 1, :] * states_ref[j, :states, :].astype(f32)
    return total


def mixed_kernel(me_ref, states_ref, c_ref, cum_ref, local_ref, table_ref, early_ref, mixed_ref, pay_ref, later_ref):
    blocks = states_ref.shape[0]
    states = c_ref.shape[1]
    me = me_ref[0]
    parts = block_sums(states_ref, states)
    source, between = iota((blocks, blocks), 0), iota((blocks, blocks), 1)
    mask = ones_where((between > source) & (between < me))
    sums = mm(mask, parts[0]) + mm(mask, parts[1]) + mm(mask, parts[2])
    which = iota((blocks, states_ref.shape[2]), 0)
    weights = jnp.where(which < me, jnp.exp(sums), 0.0)
    high, low = split2(weighted(states_ref, weights, states))
    c = c_ref[...]
    total = local_ref[...] + jnp.exp(cum_ref[...]) * (mm(c, high) + mm(c, low))
    mixed = total.astype(bf16)
    mixed_ref[...] = mixed
    experts, total_rows, features = pay_ref.shape
    capacity = table_ref.shape[0] // experts
    pay_ref[:, :capacity, :] = (
        mm(table_ref[...], mixed).astype(bf16).reshape(experts, capacity, features)
    )
    pay_ref[:, capacity:, :] = early_ref[...]
    mask = ones_where((between < source) & (between > me))
    sums = mm(mask, parts[0]) + mm(mask, parts[1]) + mm(mask, parts[2])
    later_ref[...] = jnp.where(which > me, jnp.exp(sums), 0.0)


def norm_kernel(in_ref, out_ref, raw_ref, inv_ref, gain_ref):
    peers, _, features = in_ref.shape
    capacity = raw_ref.shape[0]
    square = jnp.zeros((capacity, features), f32)
    for e in range(peers):
        piece = in_ref[e, :capacity, :].astype(f32)
        square = square + piece * piece
    inv = lax.rsqrt(jnp.sum(square, axis=1, keepdims=True) / D + epsilon)
    inv_ref[...] = jnp.broadcast_to(inv, inv_ref.shape)
    for e in range(peers):
        here = slice(e * features, (e + 1) * features)
        piece = in_ref[e, :capacity, :]
        cot = in_ref[e, capacity : 2 * capacity, :]
        gain = jnp.sum(in_ref[e, 2 * capacity :, :].astype(f32), axis=0, keepdims=True)
        gain_ref[:, here] = gain
        raw_ref[:, here] = piece
        normed = (piece.astype(f32) * inv * gain).astype(bf16)
        for j in range(out_ref.shape[0]):
            out_ref[j, :capacity, here] = normed
            out_ref[j, capacity:, here] = cot


def expert_kernel(rows_ref, in_ref, in_peer_ref, down_ref, down_peer_ref, parts_ref, mine_ref, peer_ref):
    chips, both, width = rows_ref.shape
    capacity = both // 2
    count = chips * capacity
    rows = rows_ref[:, :capacity, :].reshape(count, width)
    cot = rows_ref[:, capacity:, :].reshape(count, width)
    d_total = None
    out_total = None
    for wide, narrow, kept in ((in_ref, down_ref, mine_ref), (in_peer_ref, down_peer_ref, peer_ref)):
        hidden = mm(rows, wide[...])
        d_act = mm_nt(cot, narrow[...])
        sigmoid_h = 1.0 / (1.0 + jnp.exp(-hidden))
        activated = (hidden * sigmoid_h).astype(bf16)
        d_hidden = (d_act * sigmoid_h * (1.0 + hidden * (1.0 - sigmoid_h))).astype(bf16)
        kept[0] = activated
        kept[1] = d_hidden
        d_part = mm_nt(d_hidden, wide[...])
        out_part = mm(activated, narrow[...])
        d_total = d_part if d_total is None else d_total + d_part
        out_total = out_part if out_total is None else out_total + out_part
    parts_ref[:, :capacity, :] = d_total.astype(bf16).reshape(chips, capacity, width)
    parts_ref[:, capacity:, :] = out_total.astype(bf16).reshape(chips, capacity, width)


def return_kernel(parts_ref, raw_ref, inv_ref, gain_ref, out_ref):
    peers, both, features = out_ref.shape
    capacity = both // 2
    total = parts_ref[0].astype(f32)
    for j in range(1, parts_ref.shape[0]):
        total = total + parts_ref[j].astype(f32)
    d_rows = total[:capacity].astype(bf16).astype(f32)
    out_rows = total[capacity:]
    scaled = gain_ref[...] * d_rows
    raw = raw_ref[...].astype(f32)
    inv = inv_ref[:, 0:1]
    inner = jnp.sum(scaled * raw, axis=1, keepdims=True)
    result = inv * scaled - raw * (inv * inv * inv * inner / D)
    for e in range(peers):
        here = slice(e * features, (e + 1) * features)
        out_ref[e, :capacity, :] = result[:, here].astype(bf16)
        out_ref[e, capacity:, :] = out_rows[:, here].astype(bf16)


def block_out_kernel(rows_ref, from_ref, weight_ref, mixed_ref, out_ref):
    half = rows_ref.shape[1] // 2
    rows = rows_ref[:, half:, :].reshape(from_ref.shape[2], rows_ref.shape[2])
    total = mixed_ref[...].astype(f32)
    extra = weight_ref[:, 0:1] * mm(from_ref[0], rows) + weight_ref[:, 1:2] * mm(from_ref[1], rows)
    out_ref[...] = (total + extra).astype(bf16)


def cot_state_kernel(rows_ref, from_ref, grad_ref, c_ref, cum_ref, residual_ref, wide_ref, pay_ref):
    half = rows_ref.shape[1] // 2
    rows = rows_ref[:, :half, :].reshape(from_ref.shape[2], rows_ref.shape[2])
    table = from_ref[0] + from_ref[1]
    total = grad_ref[...].astype(f32) + mm(table, rows)
    wide_ref[...] = total
    residual_ref[...] = total.astype(bf16)
    high, low = split2(jnp.exp(cum_ref[...]) * total)
    c = c_ref[...]
    state = (mm_t(c, high) + mm_t(c, low)).astype(bf16)
    for j in range(pay_ref.shape[0]):
        pay_ref[j] = state


def back_local_kernel(wide_ref, back_ref, skip_ref, out_ref):
    tokens, features = wide_ref.shape
    heads = back_ref.shape[1]
    width = features // heads
    wide = wide_ref[...]
    high, low = split2(wide)
    lane = iota((tokens, features), 1)
    total = per_head(skip_ref[...], (1, features), width) * wide
    for head in range(heads):
        product = mm(back_ref[0, head], high) + mm(back_ref[1, head], high) + mm(back_ref[0, head], low)
        inside = (lane >= head * width) & (lane < (head + 1) * width)
        total = total + jnp.where(inside, product, 0.0)
    out_ref[...] = total


def final_kernel(states_ref, later_ref, b_ref, cum_ref, local_ref, out_ref):
    tokens = cum_ref.shape[0]
    high, low = split2(weighted(states_ref, later_ref[...], states_ref.shape[1]))
    cum = cum_ref[...]
    tail = jnp.exp(cum[tokens - 1 : tokens, :] - cum)
    b = b_ref[...]
    out_ref[...] = (local_ref[...] + tail * (mm(b, high) + mm(b, low))).astype(bf16)


def swap(a, axis, groups=None):
    return lax.all_to_all(
        a, axis, split_axis=0, concat_axis=0, tiled=True, axis_index_groups=groups
    )


def body(
    residual,
    ssd_input,
    state_in,
    state_out,
    log_decay,
    skip_gain,
    norm_gain,
    route_weight,
    expert_ids,
    weight_in,
    weight_down,
    out_grad,
):
    tokens, features = residual.shape
    heads = log_decay.shape[1]
    states = state_in.shape[1]
    experts = lax.axis_size("exp")
    blocks = lax.axis_size("ctx")
    rows = 2 * tokens
    capacity = rows // experts
    me = lax.axis_index("ctx").astype(jnp.int32).reshape(1)
    skip = skip_gain.reshape(1, heads)
    matrix_in = weight_in[0]
    matrix_down = weight_down[0]

    chips = blocks // 2
    same_core = [[2 * chip + core for chip in range(chips)] for core in range(2)]
    partners = [(i, i ^ 1) for i in range(blocks)]

    def partner(a):
        return lax.ppermute(a, "ctx", partners)

    state_pay, cum = call(
        state_kernel,
        (shape_of((blocks, states + 16, features), bf16), shape_of((tokens, features), f32)),
        ssd_input, state_in, log_decay.T,
    )
    state_all = swap(state_pay, "ctx")
    peer_in = partner(matrix_in)
    peer_down = partner(matrix_down)

    to_rows, from_rows, cot_pay = call(
        route_kernel,
        (
            shape_of((rows, tokens), bf16),
            shape_of((2, tokens, rows), bf16),
            shape_of((experts, capacity + 8, features), bf16),
        ),
        expert_ids, expert_ids.T, route_weight, out_grad, norm_gain.reshape(1, features),
    )
    local, back = call(
        local_kernel,
        (shape_of((tokens, features), f32), shape_of((2, heads, tokens, tokens), bf16)),
        ssd_input, state_in, state_out, cum, skip, residual,
    )
    mixed, rows_pay, later = call(
        mixed_kernel,
        (
            shape_of((tokens, features), bf16),
            shape_of((experts, 2 * capacity + 8, features), bf16),
            shape_of((blocks, features), f32),
        ),
        me, state_all, state_out, cum, local, to_rows, cot_pay,
        smem=(0,),
    )
    arrived = swap(rows_pay, "exp")
    spread, raw, inv, gain = call(
        norm_kernel,
        (
            shape_of((chips, 2 * capacity, D), bf16),
            shape_of((capacity, D), bf16),
            shape_of((capacity, 128), f32),
            shape_of((1, D), f32),
        ),
        arrived,
    )
    expert_rows = swap(spread, "ctx", same_core)

    units = matrix_in.shape[1]
    count = chips * capacity
    parts, mine, peer = call(
        expert_kernel,
        (
            shape_of((chips, 2 * capacity, D), bf16),
            shape_of((2, count, units), bf16),
            shape_of((2, count, units), bf16),
        ),
        expert_rows, matrix_in, peer_in, matrix_down, peer_down,
    )
    parts_all = swap(parts, "ctx", same_core)
    peer_rows = partner(expert_rows)
    peer_units = partner(peer)
    all_rows = jnp.concatenate([expert_rows[:, :capacity], peer_rows[:, :capacity]]).reshape(-1, D)
    all_cot = jnp.concatenate([expert_rows[:, capacity:], peer_rows[:, capacity:]]).reshape(-1, D)
    all_units = jnp.concatenate([mine, peer_units], axis=1)
    grad_down = mm_t(all_units[0], all_cot).astype(bf16)
    grad_in = mm_t(all_rows, all_units[1]).astype(bf16)

    back_pay = call(
        return_kernel,
        shape_of((experts, 2 * capacity, features), bf16),
        parts_all, raw, inv, gain,
    )
    returned = swap(back_pay, "exp")

    grad_residual, wide, cot_pay_state = call(
        cot_state_kernel,
        (
            shape_of((tokens, features), bf16),
            shape_of((tokens, features), f32),
            shape_of((blocks, states, features), bf16),
        ),
        returned, from_rows, out_grad, state_out, cum,
    )
    cot_states = swap(cot_pay_state, "ctx")
    back_local = call(
        back_local_kernel, shape_of((tokens, features), f32), wide, back, skip
    )
    block_out = call(
        block_out_kernel, shape_of((tokens, features), bf16), returned, from_rows, route_weight, mixed
    )
    grad_input = call(
        final_kernel, shape_of((tokens, features), bf16), cot_states, later, state_in, cum, back_local
    )
    return (block_out, grad_residual, grad_input, grad_in[None], grad_down[None])


def solution(mesh):
    placed = (
        P("ctx", "exp"),
        P("ctx", "exp"),
        P("ctx", None),
        P("ctx", None),
        P("ctx", "exp"),
        P("exp"),
        P("exp"),
        P("ctx", None),
        P("ctx", None),
        P("exp", None, "ctx"),
        P("exp", "ctx", None),
        P("ctx", "exp"),
    )
    return jax.shard_map(
        body,
        mesh=mesh,
        in_specs=placed,
        out_specs=(
            P("ctx", "exp"),
            P("ctx", "exp"),
            P("ctx", "exp"),
            P("exp", None, "ctx"),
            P("exp", "ctx", None),
        ),
        check_vma=False,
    )
```

```python
import jax
import jax.numpy as jnp
from jax import lax
from jax.experimental import pallas as pl
from jax.experimental.pallas import tpu as pltpu
from jax.sharding import PartitionSpec as P


D = 2048
epsilon = 1e-05
f32 = jnp.float32
bf16 = jnp.bfloat16


def iota(shape, axis):
    return lax.broadcasted_iota(jnp.int32, shape, axis)


def mm(a, b):
    return jnp.dot(a, b, preferred_element_type=f32)


def mm_t(a, b):
    return lax.dot_general(a, b, (((0,), (0,)), ((), ())), preferred_element_type=f32)


def mm_nt(a, b):
    return lax.dot_general(a, b, (((1,), (1,)), ((), ())), preferred_element_type=f32)


def split2(a):
    high = a.astype(bf16)
    return high, (a - high.astype(f32)).astype(bf16)


def split3(a):
    high = a.astype(bf16)
    rest = a - high.astype(f32)
    middle = rest.astype(bf16)
    return high, middle, (rest - middle.astype(f32)).astype(bf16)


def per_head(columns, shape, width):
    lane = iota(shape, 1)
    value = jnp.broadcast_to(columns[:, 0:1], shape)
    for head in range(1, columns.shape[1]):
        value = jnp.where(lane >= head * width, columns[:, head : head + 1], value)
    return value


def ones_where(condition, dtype=bf16):
    return jnp.where(condition, 1.0, 0.0).astype(dtype)


def call(kernel, outs, *args, smem=(), near=()):
    args = [
        pltpu.with_memory_space_constraint(a, pltpu.VMEM) if a.ndim > 2 or i in near else a
        for i, a in enumerate(args)
    ]
    return pl.pallas_call(
        kernel,
        out_shape=outs,
        in_specs=[
            pl.BlockSpec(memory_space=pltpu.SMEM if i in smem else pltpu.VMEM)
            for i in range(len(args))
        ],
        out_specs=jax.tree.map(lambda o: pl.BlockSpec(memory_space=pltpu.VMEM), outs),
    )(*args)


def shape_of(shape, dtype):
    return jax.ShapeDtypeStruct(shape, dtype)


def route_kernel(ids_ref, ids_t_ref, weight_ref, grad_ref, gain_ref, to_rows_ref, from_ref, pay_ref):
    tokens, features = grad_ref.shape
    experts, _, _ = pay_ref.shape
    rows = to_rows_ref.shape[0]
    capacity = rows // experts
    square = (tokens, tokens)
    grad = grad_ref[...].astype(f32)
    hits_t = [ids_t_ref[k : k + 1, :] == iota(square, 0) for k in range(2)]
    sum_t = ones_where(hits_t[0] | hits_t[1])
    before_t = mm(sum_t, ones_where(iota(square, 0) < iota(square, 1)))
    hits = [ids_ref[:, k : k + 1] == iota(square, 1) for k in range(2)]
    both = ones_where(hits[0] | hits[1])
    before = mm(ones_where(iota(square, 1) < iota(square, 0)), both)
    spread = []
    cot = jnp.zeros((rows, features), f32)
    for k in range(2):
        slot_t = jnp.sum(jnp.where(hits_t[k], before_t, 0.0), axis=0, keepdims=True)
        row_t = ids_t_ref[k : k + 1, :] * capacity + slot_t.astype(jnp.int32)
        table_t = ones_where(iota((rows, tokens), 0) == row_t)
        spread.append(table_t)
        scaled = (weight_ref[:, k : k + 1] * grad).astype(bf16)
        cot = cot + mm(table_t, scaled)
        slot = jnp.sum(jnp.where(hits[k], before, 0.0), axis=1, keepdims=True)
        row = ids_ref[:, k : k + 1] * capacity + slot.astype(jnp.int32)
        from_ref[k] = ones_where(iota((tokens, rows), 1) == row)
    to_rows_ref[...] = spread[0] + spread[1]
    pay_ref[:, :capacity, :] = cot.astype(bf16).reshape(experts, capacity, features)
    high, middle, low = split3(gain_ref[...])
    place = iota((pay_ref.shape[1] - capacity, features), 0)
    pieces = jnp.where(
        place == 0,
        high.astype(f32),
        jnp.where(place == 1, middle.astype(f32), jnp.where(place == 2, low.astype(f32), 0.0)),
    ).astype(bf16)
    pay_ref[:, capacity:, :] = jnp.broadcast_to(pieces[None], (experts,) + pieces.shape)


def state_kernel(x_ref, b_ref, decay_ref, pay_ref, cum_ref):
    tokens, features = x_ref.shape
    heads = decay_ref.shape[0]
    width = features // heads
    square = (tokens, tokens)
    place = iota((features, tokens), 0)
    spread = jnp.broadcast_to(decay_ref[0:1, :], (features, tokens))
    for head in range(1, heads):
        spread = jnp.where(place >= head * width, decay_ref[head : head + 1, :], spread)
    causal = ones_where(iota(square, 0) <= iota(square, 1))
    high, middle, low = split3(spread)
    cum = (mm(high, causal) + mm(middle, causal) + mm(low, causal)).T
    cum_ref[...] = cum
    ending = cum[tokens - 1 : tokens, :]
    tail = jnp.exp(ending - cum)
    moved_high, moved_low = split2(tail * x_ref[...].astype(f32))
    b = b_ref[...]
    state = (mm_t(b, moved_high) + mm_t(b, moved_low)).astype(bf16)
    states = state.shape[0]
    parts = split3(ending)
    place = iota((pay_ref.shape[1] - states, features), 0)
    extra = jnp.where(
        place == 0,
        parts[0].astype(f32),
        jnp.where(place == 1, parts[1].astype(f32), jnp.where(place == 2, parts[2].astype(f32), 0.0)),
    ).astype(bf16)
    for j in range(pay_ref.shape[0]):
        pay_ref[j, :states, :] = state
        pay_ref[j, states:, :] = extra


def local_kernel(x_ref, b_ref, c_ref, cum_ref, skip_ref, residual_ref, local_ref, back_ref):
    tokens, features = x_ref.shape
    heads = back_ref.shape[1]
    width = features // heads
    square = (tokens, tokens)
    x = x_ref[...]
    cum = cum_ref[...]
    cum_t = cum.T
    inner = mm_nt(c_ref[...], b_ref[...])
    inner_t = mm_nt(b_ref[...], c_ref[...])
    causal = iota(square, 1) <= iota(square, 0)
    causal_t = iota(square, 0) <= iota(square, 1)
    lane = iota((tokens, features), 1)
    skip = per_head(skip_ref[...], (1, features), width)
    total = residual_ref[...].astype(f32) + skip * x.astype(f32)
    for head in range(heads):
        column = cum[:, head * width : head * width + 1]
        row = cum_t[head * width : head * width + 1, :]
        gap = jnp.where(causal, column - row, -jnp.inf)
        high, low = split2(inner * jnp.exp(gap))
        product = mm(high, x) + mm(low, x)
        inside = (lane >= head * width) & (lane < (head + 1) * width)
        total = total + jnp.where(inside, product, 0.0)
        gap_t = jnp.where(causal_t, row - column, -jnp.inf)
        high, low = split2(inner_t * jnp.exp(gap_t))
        back_ref[0, head] = high
        back_ref[1, head] = low
    local_ref[...] = total


def block_sums(states_ref, rows_at):
    blocks = states_ref.shape[0]
    features = states_ref.shape[2]
    extra = states_ref[:, rows_at : rows_at + 16, :].astype(f32)
    place = iota((blocks, 16, features), 1)
    return [
        jnp.sum(jnp.where(place == k, extra, 0.0), axis=1).astype(bf16) for k in range(3)
    ]


def weighted(states_ref, weights, states):
    total = jnp.zeros((states, states_ref.shape[2]), f32)
    for j in range(states_ref.shape[0]):
        total = total + weights[j : j + 1, :] * states_ref[j, :states, :].astype(f32)
    return total


def mixed_kernel(me_ref, states_ref, c_ref, cum_ref, local_ref, table_ref, early_ref, mixed_ref, pay_ref, later_ref):
    blocks = states_ref.shape[0]
    states = c_ref.shape[1]
    me = me_ref[0]
    parts = block_sums(states_ref, states)
    source, between = iota((blocks, blocks), 0), iota((blocks, blocks), 1)
    mask = ones_where((between > source) & (between < me))
    sums = mm(mask, parts[0]) + mm(mask, parts[1]) + mm(mask, parts[2])
    which = iota((blocks, states_ref.shape[2]), 0)
    weights = jnp.where(which < me, jnp.exp(sums), 0.0)
    high, low = split2(weighted(states_ref, weights, states))
    c = c_ref[...]
    total = local_ref[...] + jnp.exp(cum_ref[...]) * (mm(c, high) + mm(c, low))
    mixed = total.astype(bf16)
    mixed_ref[...] = mixed
    experts, _, features = pay_ref.shape
    capacity = table_ref.shape[0] // experts
    pay_ref[:, :capacity, :] = (
        mm(table_ref[...], mixed).astype(bf16).reshape(experts, capacity, features)
    )
    pay_ref[:, capacity:, :] = early_ref[...]
    mask = ones_where((between < source) & (between > me))
    sums = mm(mask, parts[0]) + mm(mask, parts[1]) + mm(mask, parts[2])
    later_ref[...] = jnp.where(which > me, jnp.exp(sums), 0.0)


def norm_kernel(in_ref, out_ref, raw_ref, inv_ref, gain_ref):
    peers, _, features = in_ref.shape
    capacity = raw_ref.shape[0]
    square = jnp.zeros((capacity, features), f32)
    for e in range(peers):
        piece = in_ref[e, :capacity, :].astype(f32)
        square = square + piece * piece
    inv = lax.rsqrt(jnp.sum(square, axis=1, keepdims=True) / D + epsilon)
    inv_ref[...] = jnp.broadcast_to(inv, inv_ref.shape)
    for e in range(peers):
        here = slice(e * features, (e + 1) * features)
        piece = in_ref[e, :capacity, :]
        cot = in_ref[e, capacity : 2 * capacity, :]
        gain = jnp.sum(in_ref[e, 2 * capacity :, :].astype(f32), axis=0, keepdims=True)
        gain_ref[:, here] = gain
        raw_ref[:, here] = piece
        normed = (piece.astype(f32) * inv * gain).astype(bf16)
        for j in range(out_ref.shape[0]):
            out_ref[j, :capacity, here] = normed
            out_ref[j, capacity:, here] = cot


def expert_kernel(*refs):
    rows_ref = refs[0]
    weights = refs[1:9]
    parts_ref = refs[9]
    units = refs[10:14]
    held = refs[14:22]
    sems = refs[22]
    copies = [
        pltpu.make_async_copy(source, target, sems.at[k])
        for k, (source, target) in enumerate(zip(weights, held))
    ]
    for copy in copies:
        copy.start()
    chips, both, width = rows_ref.shape
    capacity = both // 2
    count = chips * capacity
    rows = rows_ref[:, :capacity, :].reshape(count, width)
    cot = rows_ref[:, capacity:, :].reshape(count, width)
    d_total = None
    out_total = None
    for k in range(4):
        copies[2 * k].wait()
        copies[2 * k + 1].wait()
        wide = held[2 * k][...]
        narrow = held[2 * k + 1][...]
        hidden = mm(rows, wide)
        d_act = mm_nt(cot, narrow)
        sigmoid_h = 1.0 / (1.0 + jnp.exp(-hidden))
        activated = (hidden * sigmoid_h).astype(bf16)
        d_hidden = (d_act * sigmoid_h * (1.0 + hidden * (1.0 - sigmoid_h))).astype(bf16)
        units[k][0] = activated
        units[k][1] = d_hidden
        d_part = mm_nt(d_hidden, wide)
        out_part = mm(activated, narrow)
        d_total = d_part if d_total is None else d_total + d_part
        out_total = out_part if out_total is None else out_total + out_part
    parts_ref[:, :capacity, :] = d_total.astype(bf16).reshape(chips, capacity, width)
    parts_ref[:, capacity:, :] = out_total.astype(bf16).reshape(chips, capacity, width)


def run_experts(rows, weights):
    chips, both, _ = rows.shape
    units = weights[0].shape[1]
    count = chips * both // 2
    near = pl.BlockSpec(memory_space=pltpu.VMEM)
    kept = [shape_of((2, count, units), bf16)] * 4
    return pl.pallas_call(
        expert_kernel,
        out_shape=[shape_of(rows.shape, bf16)] + kept,
        in_specs=[near] + [pl.BlockSpec(memory_space=pl.ANY)] * 8,
        out_specs=[near] * 5,
        scratch_shapes=[pltpu.VMEM(w.shape, bf16) for w in weights]
        + [pltpu.SemaphoreType.DMA((8,))],
    )(pltpu.with_memory_space_constraint(rows, pltpu.VMEM), *weights)


def return_kernel(parts_ref, raw_ref, inv_ref, gain_ref, out_ref):
    peers, both, features = out_ref.shape
    capacity = both // 2
    total = parts_ref[0].astype(f32)
    for j in range(1, parts_ref.shape[0]):
        total = total + parts_ref[j].astype(f32)
    d_rows = total[:capacity].astype(bf16).astype(f32)
    out_rows = total[capacity:]
    scaled = gain_ref[...] * d_rows
    raw = raw_ref[...].astype(f32)
    inv = inv_ref[:, 0:1]
    inner = jnp.sum(scaled * raw, axis=1, keepdims=True)
    result = inv * scaled - raw * (inv * inv * inv * inner / D)
    for e in range(peers):
        here = slice(e * features, (e + 1) * features)
        out_ref[e, :capacity, :] = result[:, here].astype(bf16)
        out_ref[e, capacity:, :] = out_rows[:, here].astype(bf16)


def block_out_kernel(rows_ref, from_ref, weight_ref, mixed_ref, out_ref):
    half = rows_ref.shape[1] // 2
    rows = rows_ref[:, half:, :].reshape(from_ref.shape[2], rows_ref.shape[2])
    total = mixed_ref[...].astype(f32)
    extra = weight_ref[:, 0:1] * mm(from_ref[0], rows) + weight_ref[:, 1:2] * mm(from_ref[1], rows)
    out_ref[...] = (total + extra).astype(bf16)


def cot_state_kernel(rows_ref, from_ref, grad_ref, c_ref, cum_ref, residual_ref, wide_ref, pay_ref):
    half = rows_ref.shape[1] // 2
    rows = rows_ref[:, :half, :].reshape(from_ref.shape[2], rows_ref.shape[2])
    table = from_ref[0] + from_ref[1]
    total = grad_ref[...].astype(f32) + mm(table, rows)
    wide_ref[...] = total
    residual_ref[...] = total.astype(bf16)
    high, low = split2(jnp.exp(cum_ref[...]) * total)
    c = c_ref[...]
    state = (mm_t(c, high) + mm_t(c, low)).astype(bf16)
    for j in range(pay_ref.shape[0]):
        pay_ref[j] = state


def back_local_kernel(wide_ref, back_ref, skip_ref, out_ref):
    tokens, features = wide_ref.shape
    heads = back_ref.shape[1]
    width = features // heads
    wide = wide_ref[...]
    high, low = split2(wide)
    lane = iota((tokens, features), 1)
    total = per_head(skip_ref[...], (1, features), width) * wide
    for head in range(heads):
        product = mm(back_ref[0, head], high) + mm(back_ref[1, head], high) + mm(back_ref[0, head], low)
        inside = (lane >= head * width) & (lane < (head + 1) * width)
        total = total + jnp.where(inside, product, 0.0)
    out_ref[...] = total


def final_kernel(states_ref, later_ref, b_ref, cum_ref, local_ref, out_ref):
    tokens = cum_ref.shape[0]
    high, low = split2(weighted(states_ref, later_ref[...], states_ref.shape[1]))
    cum = cum_ref[...]
    tail = jnp.exp(cum[tokens - 1 : tokens, :] - cum)
    b = b_ref[...]
    out_ref[...] = (local_ref[...] + tail * (mm(b, high) + mm(b, low))).astype(bf16)


def swap(a, axis, groups=None):
    return lax.all_to_all(
        a, axis, split_axis=0, concat_axis=0, tiled=True, axis_index_groups=groups
    )


def body(
    residual,
    ssd_input,
    state_in,
    state_out,
    log_decay,
    skip_gain,
    norm_gain,
    route_weight,
    expert_ids,
    weight_in,
    weight_down,
    out_grad,
):
    tokens, features = residual.shape
    heads = log_decay.shape[1]
    states = state_in.shape[1]
    experts = lax.axis_size("exp")
    blocks = lax.axis_size("ctx")
    rows = 2 * tokens
    capacity = rows // experts
    me = lax.axis_index("ctx").astype(jnp.int32).reshape(1)
    skip = skip_gain.reshape(1, heads)
    matrix_in = weight_in[0]
    matrix_down = weight_down[0]

    chips = [(x, y) for x in range(4) for y in range(4)]

    def place(x, y, core):
        return x * 8 + y * 2 + core

    colours = [
        [place(x, y, core) for x, y in chips if (x + y) % 2 == colour]
        for core in range(2)
        for colour in range(2)
    ]
    members = len(colours[0])
    near_of = {}
    for x, y in chips:
        near_of[place(x, y, 0)] = place(x ^ 1, y, 0)
        near_of[place(x, y, 1)] = place(x, y ^ 1, 1)

    def partner(a):
        return lax.ppermute(a, "ctx", [(i, i ^ 1) for i in range(blocks)])

    def near(a):
        return lax.ppermute(a, "ctx", [(i, near_of[i]) for i in range(blocks)])

    def across(a):
        return lax.ppermute(a, "ctx", [(i, near_of[i ^ 1]) for i in range(blocks)])

    state_pay, cum = call(
        state_kernel,
        (shape_of((blocks, states + 16, features), bf16), shape_of((tokens, features), f32)),
        ssd_input, state_in, log_decay.T,
    )
    state_all = swap(state_pay, "ctx")
    near_in = near(matrix_in)
    near_down = near(matrix_down)
    peer_in = partner(matrix_in)
    peer_down = partner(matrix_down)
    far_in = partner(near_in)
    far_down = partner(near_down)

    to_rows, from_rows, cot_pay = call(
        route_kernel,
        (
            shape_of((rows, tokens), bf16),
            shape_of((2, tokens, rows), bf16),
            shape_of((experts, capacity + 8, features), bf16),
        ),
        expert_ids, expert_ids.T, route_weight, out_grad, norm_gain.reshape(1, features),
    )
    local, back = call(
        local_kernel,
        (shape_of((tokens, features), f32), shape_of((2, heads, tokens, tokens), bf16)),
        ssd_input, state_in, state_out, cum, skip, residual,
    )
    mixed, rows_pay, later = call(
        mixed_kernel,
        (
            shape_of((tokens, features), bf16),
            shape_of((experts, 2 * capacity + 8, features), bf16),
            shape_of((blocks, features), f32),
        ),
        me, state_all, state_out, cum, local, to_rows, cot_pay,
        smem=(0,),
    )
    arrived = swap(rows_pay, "exp")
    spread, raw, inv, gain = call(
        norm_kernel,
        (
            shape_of((members, 2 * capacity, D), bf16),
            shape_of((capacity, D), bf16),
            shape_of((capacity, 128), f32),
            shape_of((1, D), f32),
        ),
        arrived,
    )
    expert_rows = swap(spread, "ctx", colours)

    parts, mine, of_peer, of_near, of_far = run_experts(
        expert_rows,
        (matrix_in, matrix_down, peer_in, peer_down, near_in, near_down, far_in, far_down),
    )
    parts_all = swap(parts, "ctx", colours)
    peer_rows = partner(expert_rows)
    near_rows = near(expert_rows)
    far_rows = near(peer_rows)
    units = (mine, partner(of_peer), near(of_near), across(of_far))
    lots = (expert_rows, peer_rows, near_rows, far_rows)
    all_rows = jnp.concatenate([lot[:, :capacity] for lot in lots]).reshape(-1, D)
    all_cot = jnp.concatenate([lot[:, capacity:] for lot in lots]).reshape(-1, D)
    all_units = jnp.concatenate(units, axis=1)
    grad_down = mm_t(all_units[0], all_cot).astype(bf16)
    grad_in = mm_t(all_rows, all_units[1]).astype(bf16)

    back_pay = call(
        return_kernel,
        shape_of((experts, 2 * capacity, features), bf16),
        parts_all, raw, inv, gain,
    )
    returned = swap(back_pay, "exp")

    grad_residual, wide, cot_pay_state = call(
        cot_state_kernel,
        (
            shape_of((tokens, features), bf16),
            shape_of((tokens, features), f32),
            shape_of((blocks, states, features), bf16),
        ),
        returned, from_rows, out_grad, state_out, cum,
    )
    cot_states = swap(cot_pay_state, "ctx")
    back_local = call(
        back_local_kernel, shape_of((tokens, features), f32), wide, back, skip
    )
    block_out = call(
        block_out_kernel, shape_of((tokens, features), bf16), returned, from_rows, route_weight, mixed
    )
    grad_input = call(
        final_kernel, shape_of((tokens, features), bf16), cot_states, later, state_in, cum, back_local
    )
    return (block_out, grad_residual, grad_input, grad_in[None], grad_down[None])


def solution(mesh):
    placed = (
        P("ctx", "exp"),
        P("ctx", "exp"),
        P("ctx", None),
        P("ctx", None),
        P("ctx", "exp"),
        P("exp"),
        P("exp"),
        P("ctx", None),
        P("ctx", None),
        P("exp", None, "ctx"),
        P("exp", "ctx", None),
        P("ctx", "exp"),
    )
    return jax.shard_map(
        body,
        mesh=mesh,
        in_specs=placed,
        out_specs=(
            P("ctx", "exp"),
            P("ctx", "exp"),
            P("ctx", "exp"),
            P("exp", None, "ctx"),
            P("exp", "ctx", None),
        ),
        check_vma=False,
    )
```

```python
import jax
import jax.numpy as jnp
from jax import lax
from jax.experimental import pallas as pl
from jax.experimental.pallas import tpu as pltpu
from jax.sharding import PartitionSpec as P


D = 2048
epsilon = 1e-05
f32 = jnp.float32
bf16 = jnp.bfloat16


def iota(shape, axis):
    return lax.broadcasted_iota(jnp.int32, shape, axis)


def mm(a, b):
    return jnp.dot(a, b, preferred_element_type=f32)


def mm_t(a, b):
    return lax.dot_general(a, b, (((0,), (0,)), ((), ())), preferred_element_type=f32)


def mm_nt(a, b):
    return lax.dot_general(a, b, (((1,), (1,)), ((), ())), preferred_element_type=f32)


def split2(a):
    high = a.astype(bf16)
    return high, (a - high.astype(f32)).astype(bf16)


def split3(a):
    high = a.astype(bf16)
    rest = a - high.astype(f32)
    middle = rest.astype(bf16)
    return high, middle, (rest - middle.astype(f32)).astype(bf16)


def per_head(columns, shape, width):
    lane = iota(shape, 1)
    value = jnp.broadcast_to(columns[:, 0:1], shape)
    for head in range(1, columns.shape[1]):
        value = jnp.where(lane >= head * width, columns[:, head : head + 1], value)
    return value


def ones_where(condition, dtype=bf16):
    return jnp.where(condition, 1.0, 0.0).astype(dtype)


def call(kernel, outs, *args, smem=(), near=()):
    args = [
        pltpu.with_memory_space_constraint(a, pltpu.VMEM)
        if near is not None and (a.ndim > 2 or i in near)
        else a
        for i, a in enumerate(args)
    ]
    return pl.pallas_call(
        kernel,
        out_shape=outs,
        in_specs=[
            pl.BlockSpec(memory_space=pltpu.SMEM if i in smem else pltpu.VMEM)
            for i in range(len(args))
        ],
        out_specs=jax.tree.map(lambda o: pl.BlockSpec(memory_space=pltpu.VMEM), outs),
    )(*args)


def shape_of(shape, dtype):
    return jax.ShapeDtypeStruct(shape, dtype)


def route_kernel(ids_ref, ids_t_ref, weight_ref, grad_ref, gain_ref, to_rows_ref, from_ref, pay_ref):
    tokens, features = grad_ref.shape
    experts, _, _ = pay_ref.shape
    rows = to_rows_ref.shape[0]
    capacity = rows // experts
    square = (tokens, tokens)
    grad = grad_ref[...].astype(f32)
    hits_t = [ids_t_ref[k : k + 1, :] == iota(square, 0) for k in range(2)]
    sum_t = ones_where(hits_t[0] | hits_t[1])
    before_t = mm(sum_t, ones_where(iota(square, 0) < iota(square, 1)))
    hits = [ids_ref[:, k : k + 1] == iota(square, 1) for k in range(2)]
    both = ones_where(hits[0] | hits[1])
    before = mm(ones_where(iota(square, 1) < iota(square, 0)), both)
    spread = []
    cot = jnp.zeros((rows, features), f32)
    for k in range(2):
        slot_t = jnp.sum(jnp.where(hits_t[k], before_t, 0.0), axis=0, keepdims=True)
        row_t = ids_t_ref[k : k + 1, :] * capacity + slot_t.astype(jnp.int32)
        table_t = ones_where(iota((rows, tokens), 0) == row_t)
        spread.append(table_t)
        scaled = (weight_ref[:, k : k + 1] * grad).astype(bf16)
        cot = cot + mm(table_t, scaled)
        slot = jnp.sum(jnp.where(hits[k], before, 0.0), axis=1, keepdims=True)
        row = ids_ref[:, k : k + 1] * capacity + slot.astype(jnp.int32)
        from_ref[k] = ones_where(iota((tokens, rows), 1) == row)
    to_rows_ref[...] = spread[0] + spread[1]
    pay_ref[:, :capacity, :] = cot.astype(bf16).reshape(experts, capacity, features)
    high, middle, low = split3(gain_ref[...])
    place = iota((pay_ref.shape[1] - capacity, features), 0)
    pieces = jnp.where(
        place == 0,
        high.astype(f32),
        jnp.where(place == 1, middle.astype(f32), jnp.where(place == 2, low.astype(f32), 0.0)),
    ).astype(bf16)
    pay_ref[:, capacity:, :] = jnp.broadcast_to(pieces[None], (experts,) + pieces.shape)


def state_kernel(x_ref, b_ref, decay_ref, pay_ref, cum_ref):
    tokens, features = x_ref.shape
    heads = decay_ref.shape[0]
    width = features // heads
    square = (tokens, tokens)
    place = iota((features, tokens), 0)
    spread = jnp.broadcast_to(decay_ref[0:1, :], (features, tokens))
    for head in range(1, heads):
        spread = jnp.where(place >= head * width, decay_ref[head : head + 1, :], spread)
    causal = ones_where(iota(square, 0) <= iota(square, 1))
    high, middle, low = split3(spread)
    cum = (mm(high, causal) + mm(middle, causal) + mm(low, causal)).T
    cum_ref[...] = cum
    ending = cum[tokens - 1 : tokens, :]
    tail = jnp.exp(ending - cum)
    moved_high, moved_low = split2(tail * x_ref[...].astype(f32))
    b = b_ref[...]
    state = (mm_t(b, moved_high) + mm_t(b, moved_low)).astype(bf16)
    states = state.shape[0]
    parts = split3(ending)
    place = iota((pay_ref.shape[1] - states, features), 0)
    extra = jnp.where(
        place == 0,
        parts[0].astype(f32),
        jnp.where(place == 1, parts[1].astype(f32), jnp.where(place == 2, parts[2].astype(f32), 0.0)),
    ).astype(bf16)
    for j in range(pay_ref.shape[0]):
        pay_ref[j, :states, :] = state
        pay_ref[j, states:, :] = extra


def local_kernel(x_ref, b_ref, c_ref, cum_ref, skip_ref, residual_ref, local_ref, back_ref):
    tokens, features = x_ref.shape
    heads = back_ref.shape[1]
    width = features // heads
    square = (tokens, tokens)
    x = x_ref[...]
    cum = cum_ref[...]
    cum_t = cum.T
    inner = mm_nt(c_ref[...], b_ref[...])
    inner_t = mm_nt(b_ref[...], c_ref[...])
    causal = iota(square, 1) <= iota(square, 0)
    causal_t = iota(square, 0) <= iota(square, 1)
    lane = iota((tokens, features), 1)
    skip = per_head(skip_ref[...], (1, features), width)
    total = residual_ref[...].astype(f32) + skip * x.astype(f32)
    for head in range(heads):
        column = cum[:, head * width : head * width + 1]
        row = cum_t[head * width : head * width + 1, :]
        gap = jnp.where(causal, column - row, -jnp.inf)
        high, low = split2(inner * jnp.exp(gap))
        product = mm(high, x) + mm(low, x)
        inside = (lane >= head * width) & (lane < (head + 1) * width)
        total = total + jnp.where(inside, product, 0.0)
        gap_t = jnp.where(causal_t, row - column, -jnp.inf)
        high, low = split2(inner_t * jnp.exp(gap_t))
        back_ref[0, head] = high
        back_ref[1, head] = low
    local_ref[...] = total


def block_sums(states_ref, rows_at):
    blocks = states_ref.shape[0]
    features = states_ref.shape[2]
    extra = states_ref[:, rows_at : rows_at + 16, :].astype(f32)
    place = iota((blocks, 16, features), 1)
    return [
        jnp.sum(jnp.where(place == k, extra, 0.0), axis=1).astype(bf16) for k in range(3)
    ]


def weighted(states_ref, weights, states):
    total = jnp.zeros((states, states_ref.shape[2]), f32)
    for j in range(states_ref.shape[0]):
        total = total + weights[j : j + 1, :] * states_ref[j, :states, :].astype(f32)
    return total


def mixed_kernel(me_ref, states_ref, c_ref, cum_ref, local_ref, table_ref, early_ref, mixed_ref, pay_ref, later_ref):
    blocks = states_ref.shape[0]
    states = c_ref.shape[1]
    me = me_ref[0]
    parts = block_sums(states_ref, states)
    source, between = iota((blocks, blocks), 0), iota((blocks, blocks), 1)
    mask = ones_where((between > source) & (between < me))
    sums = mm(mask, parts[0]) + mm(mask, parts[1]) + mm(mask, parts[2])
    which = iota((blocks, states_ref.shape[2]), 0)
    weights = jnp.where(which < me, jnp.exp(sums), 0.0)
    high, low = split2(weighted(states_ref, weights, states))
    c = c_ref[...]
    total = local_ref[...] + jnp.exp(cum_ref[...]) * (mm(c, high) + mm(c, low))
    mixed = total.astype(bf16)
    mixed_ref[...] = mixed
    experts, _, features = pay_ref.shape
    capacity = table_ref.shape[0] // experts
    pay_ref[:, :capacity, :] = (
        mm(table_ref[...], mixed).astype(bf16).reshape(experts, capacity, features)
    )
    pay_ref[:, capacity:, :] = early_ref[...]
    mask = ones_where((between < source) & (between > me))
    sums = mm(mask, parts[0]) + mm(mask, parts[1]) + mm(mask, parts[2])
    later_ref[...] = jnp.where(which > me, jnp.exp(sums), 0.0)


def norm_kernel(in_ref, out_ref, raw_ref, inv_ref, gain_ref):
    peers, _, features = in_ref.shape
    capacity = raw_ref.shape[0]
    square = jnp.zeros((capacity, features), f32)
    for e in range(peers):
        piece = in_ref[e, :capacity, :].astype(f32)
        square = square + piece * piece
    inv = lax.rsqrt(jnp.sum(square, axis=1, keepdims=True) / D + epsilon)
    inv_ref[...] = jnp.broadcast_to(inv, inv_ref.shape)
    for e in range(peers):
        here = slice(e * features, (e + 1) * features)
        piece = in_ref[e, :capacity, :]
        cot = in_ref[e, capacity : 2 * capacity, :]
        gain = jnp.sum(in_ref[e, 2 * capacity :, :].astype(f32), axis=0, keepdims=True)
        gain_ref[:, here] = gain
        raw_ref[:, here] = piece
        normed = (piece.astype(f32) * inv * gain).astype(bf16)
        for j in range(out_ref.shape[0]):
            out_ref[j, :capacity, here] = normed
            out_ref[j, capacity:, here] = cot


def pack_kernel(in_ref, down_ref, out_ref):
    units = down_ref.shape[0]
    for k in range(in_ref.shape[0] // units):
        here = slice(k * units, (k + 1) * units)
        out_ref[0, :, here] = in_ref[here, :]
    out_ref[1] = down_ref[...]


def pack_units(out_ref, lot, activated, d_hidden):
    units = activated.shape[1]
    capacity = out_ref.shape[1] // 2
    for k in range(activated.shape[0] // capacity):
        rows = slice(k * capacity, (k + 1) * capacity)
        here = slice(k * units, (k + 1) * units)
        out_ref[lot, :capacity, here] = activated[rows, :]
        out_ref[lot, capacity:, here] = d_hidden[rows, :]


def expert_kernel(rows_ref, own_ref, peer_ref, near_ref, far_ref, parts_ref, mine_ref, send_ref, held, sems):
    copies = [
        pltpu.make_async_copy(source, held.at[k], sems.at[k])
        for k, source in enumerate((own_ref, peer_ref, near_ref, far_ref))
    ]
    for copy in copies:
        copy.start()
    chips, both, width = rows_ref.shape
    capacity = both // 2
    count = chips * capacity
    units = held.shape[2]
    blocks = [slice(k * units, (k + 1) * units) for k in range(width // units)]
    rows = rows_ref[:, :capacity, :].reshape(count, width)
    cot = rows_ref[:, capacity:, :].reshape(count, width)
    send_ref[:chips] = rows_ref[...]
    d_total = [None] * len(blocks)
    out_total = None
    for k in range(4):
        copies[k].wait()
        wide = [held[k, 0, :, here] for here in blocks]
        narrow = held[k, 1]
        hidden = mm(rows[:, blocks[0]], wide[0])
        for here, piece in zip(blocks[1:], wide[1:]):
            hidden = hidden + mm(rows[:, here], piece)
        d_act = mm_nt(cot, narrow)
        sigmoid_h = 1.0 / (1.0 + jnp.exp(-hidden))
        activated = (hidden * sigmoid_h).astype(bf16)
        d_hidden = (d_act * sigmoid_h * (1.0 + hidden * (1.0 - sigmoid_h))).astype(bf16)
        if k == 0:
            mine_ref[0] = activated
            mine_ref[1] = d_hidden
        else:
            pack_units(send_ref, chips + k - 1, activated, d_hidden)
        d_part = [mm_nt(d_hidden, piece) for piece in wide]
        out_part = mm(activated, narrow)
        d_total = d_part if k == 0 else [a + b for a, b in zip(d_total, d_part)]
        out_total = out_part if k == 0 else out_total + out_part
    for here, piece in zip(blocks, d_total):
        parts_ref[:, :capacity, here] = piece.astype(bf16).reshape(chips, capacity, units)
    parts_ref[:, capacity:, :] = out_total.astype(bf16).reshape(chips, capacity, width)


def run_experts(rows, weights):
    chips, both, width = rows.shape
    units = weights[0].shape[1]
    count = chips * both // 2
    near = pl.BlockSpec(memory_space=pltpu.VMEM)
    return pl.pallas_call(
        expert_kernel,
        out_shape=[
            shape_of(rows.shape, bf16),
            shape_of((2, count, units), bf16),
            shape_of((chips + 3, both, width), bf16),
        ],
        in_specs=[near] + [pl.BlockSpec(memory_space=pl.ANY)] * 4,
        out_specs=[near] * 3,
        scratch_shapes=[
            pltpu.VMEM((4,) + weights[0].shape, bf16),
            pltpu.SemaphoreType.DMA((4,)),
        ],
    )(pltpu.with_memory_space_constraint(rows, pltpu.VMEM), *weights)


def weight_grad_kernel(own_ref, mine_ref, peer_ref, near_ref, far_ref, in_ref, down_ref):
    chips, both, width = own_ref.shape
    capacity = both // 2
    count = chips * capacity
    units = mine_ref.shape[2]
    lots = [own_ref, peer_ref, near_ref, far_ref]
    rows = jnp.concatenate([lot[:chips, :capacity, :].reshape(count, width) for lot in lots])
    cot = jnp.concatenate([lot[:chips, capacity:, :].reshape(count, width) for lot in lots])
    activated = [mine_ref[0]]
    d_hidden = [mine_ref[1]]
    for k, lot in enumerate(lots[1:]):
        for j in range(count // capacity):
            here = slice(j * units, (j + 1) * units)
            activated.append(lot[chips + k, :capacity, here])
            d_hidden.append(lot[chips + k, capacity:, here])
    in_ref[...] = mm_t(rows, jnp.concatenate(d_hidden)).astype(bf16)
    down_ref[...] = mm_t(jnp.concatenate(activated), cot).astype(bf16)


def return_kernel(parts_ref, raw_ref, inv_ref, gain_ref, out_ref):
    peers, both, features = out_ref.shape
    capacity = both // 2
    total = parts_ref[0].astype(f32)
    for j in range(1, parts_ref.shape[0]):
        total = total + parts_ref[j].astype(f32)
    d_rows = total[:capacity].astype(bf16).astype(f32)
    out_rows = total[capacity:]
    scaled = gain_ref[...] * d_rows
    raw = raw_ref[...].astype(f32)
    inv = inv_ref[:, 0:1]
    inner = jnp.sum(scaled * raw, axis=1, keepdims=True)
    result = inv * scaled - raw * (inv * inv * inv * inner / D)
    for e in range(peers):
        here = slice(e * features, (e + 1) * features)
        out_ref[e, :capacity, :] = result[:, here].astype(bf16)
        out_ref[e, capacity:, :] = out_rows[:, here].astype(bf16)


def block_out_kernel(rows_ref, from_ref, weight_ref, mixed_ref, out_ref):
    half = rows_ref.shape[1] // 2
    rows = rows_ref[:, half:, :].reshape(from_ref.shape[2], rows_ref.shape[2])
    total = mixed_ref[...].astype(f32)
    extra = weight_ref[:, 0:1] * mm(from_ref[0], rows) + weight_ref[:, 1:2] * mm(from_ref[1], rows)
    out_ref[...] = (total + extra).astype(bf16)


def cot_state_kernel(rows_ref, from_ref, grad_ref, c_ref, cum_ref, residual_ref, wide_ref, pay_ref):
    half = rows_ref.shape[1] // 2
    rows = rows_ref[:, :half, :].reshape(from_ref.shape[2], rows_ref.shape[2])
    table = from_ref[0] + from_ref[1]
    total = grad_ref[...].astype(f32) + mm(table, rows)
    wide_ref[...] = total
    residual_ref[...] = total.astype(bf16)
    high, low = split2(jnp.exp(cum_ref[...]) * total)
    c = c_ref[...]
    state = (mm_t(c, high) + mm_t(c, low)).astype(bf16)
    for j in range(pay_ref.shape[0]):
        pay_ref[j] = state


def back_local_kernel(wide_ref, back_ref, skip_ref, out_ref):
    tokens, features = wide_ref.shape
    heads = back_ref.shape[1]
    width = features // heads
    wide = wide_ref[...]
    high, low = split2(wide)
    lane = iota((tokens, features), 1)
    total = per_head(skip_ref[...], (1, features), width) * wide
    for head in range(heads):
        product = mm(back_ref[0, head], high) + mm(back_ref[1, head], high) + mm(back_ref[0, head], low)
        inside = (lane >= head * width) & (lane < (head + 1) * width)
        total = total + jnp.where(inside, product, 0.0)
    out_ref[...] = total


def final_kernel(states_ref, later_ref, b_ref, cum_ref, local_ref, out_ref):
    tokens = cum_ref.shape[0]
    high, low = split2(weighted(states_ref, later_ref[...], states_ref.shape[1]))
    cum = cum_ref[...]
    tail = jnp.exp(cum[tokens - 1 : tokens, :] - cum)
    b = b_ref[...]
    out_ref[...] = (local_ref[...] + tail * (mm(b, high) + mm(b, low))).astype(bf16)


def swap(a, axis, groups=None):
    return lax.all_to_all(
        a, axis, split_axis=0, concat_axis=0, tiled=True, axis_index_groups=groups
    )


def body(
    residual,
    ssd_input,
    state_in,
    state_out,
    log_decay,
    skip_gain,
    norm_gain,
    route_weight,
    expert_ids,
    weight_in,
    weight_down,
    out_grad,
):
    tokens, features = residual.shape
    heads = log_decay.shape[1]
    states = state_in.shape[1]
    experts = lax.axis_size("exp")
    blocks = lax.axis_size("ctx")
    rows = 2 * tokens
    capacity = rows // experts
    me = lax.axis_index("ctx").astype(jnp.int32).reshape(1)
    skip = skip_gain.reshape(1, heads)
    matrix_in = weight_in[0]
    matrix_down = weight_down[0]

    chips = [(x, y) for x in range(4) for y in range(4)]

    def place(x, y, core):
        return x * 8 + y * 2 + core

    colours = [
        [place(x, y, core) for x, y in chips if (x + y) % 2 == colour]
        for core in range(2)
        for colour in range(2)
    ]
    members = len(colours[0])
    near_of = {}
    for x, y in chips:
        near_of[place(x, y, 0)] = place(x ^ 1, y, 0)
        near_of[place(x, y, 1)] = place(x, y ^ 1, 1)

    def partner(a):
        return lax.ppermute(a, "ctx", [(i, i ^ 1) for i in range(blocks)])

    def near(a):
        return lax.ppermute(a, "ctx", [(i, near_of[i]) for i in range(blocks)])

    state_pay, cum = call(
        state_kernel,
        (shape_of((blocks, states + 16, features), bf16), shape_of((tokens, features), f32)),
        ssd_input, state_in, log_decay.T,
    )
    state_all = swap(state_pay, "ctx")
    own_w = call(
        pack_kernel, shape_of((2,) + matrix_down.shape, bf16), matrix_in, matrix_down
    )
    near_w = near(own_w)
    peer_w = partner(own_w)
    far_w = partner(near_w)

    to_rows, from_rows, cot_pay = call(
        route_kernel,
        (
            shape_of((rows, tokens), bf16),
            shape_of((2, tokens, rows), bf16),
            shape_of((experts, capacity + 8, features), bf16),
        ),
        expert_ids, expert_ids.T, route_weight, out_grad, norm_gain.reshape(1, features),
    )
    local, back = call(
        local_kernel,
        (shape_of((tokens, features), f32), shape_of((2, heads, tokens, tokens), bf16)),
        ssd_input, state_in, state_out, cum, skip, residual,
    )
    mixed, rows_pay, later = call(
        mixed_kernel,
        (
            shape_of((tokens, features), bf16),
            shape_of((experts, 2 * capacity + 8, features), bf16),
            shape_of((blocks, features), f32),
        ),
        me, state_all, state_out, cum, local, to_rows, cot_pay,
        smem=(0,),
    )
    arrived = swap(rows_pay, "exp")
    spread, raw, inv, gain = call(
        norm_kernel,
        (
            shape_of((members, 2 * capacity, D), bf16),
            shape_of((capacity, D), bf16),
            shape_of((capacity, 128), f32),
            shape_of((1, D), f32),
        ),
        arrived,
    )
    expert_rows = swap(spread, "ctx", colours)

    parts, mine, send = run_experts(expert_rows, (own_w, peer_w, near_w, far_w))
    parts_all = swap(parts, "ctx", colours)
    peer_lot = partner(send)
    near_lot = near(send)
    far_lot = near(peer_lot)
    grad_in, grad_down = call(
        weight_grad_kernel,
        (shape_of(matrix_in.shape, bf16), shape_of(matrix_down.shape, bf16)),
        expert_rows, mine, peer_lot, near_lot, far_lot,
        near=None,
    )

    back_pay = call(
        return_kernel,
        shape_of((experts, 2 * capacity, features), bf16),
        parts_all, raw, inv, gain,
    )
    returned = swap(back_pay, "exp")

    grad_residual, wide, cot_pay_state = call(
        cot_state_kernel,
        (
            shape_of((tokens, features), bf16),
            shape_of((tokens, features), f32),
            shape_of((blocks, states, features), bf16),
        ),
        returned, from_rows, out_grad, state_out, cum,
    )
    cot_states = swap(cot_pay_state, "ctx")
    back_local = call(
        back_local_kernel, shape_of((tokens, features), f32), wide, back, skip
    )
    block_out = call(
        block_out_kernel, shape_of((tokens, features), bf16), returned, from_rows, route_weight, mixed
    )
    grad_input = call(
        final_kernel, shape_of((tokens, features), bf16), cot_states, later, state_in, cum, back_local
    )
    return (block_out, grad_residual, grad_input, grad_in[None], grad_down[None])


def solution(mesh):
    placed = (
        P("ctx", "exp"),
        P("ctx", "exp"),
        P("ctx", None),
        P("ctx", None),
        P("ctx", "exp"),
        P("exp"),
        P("exp"),
        P("ctx", None),
        P("ctx", None),
        P("exp", None, "ctx"),
        P("exp", "ctx", None),
        P("ctx", "exp"),
    )
    return jax.shard_map(
        body,
        mesh=mesh,
        in_specs=placed,
        out_specs=(
            P("ctx", "exp"),
            P("ctx", "exp"),
            P("ctx", "exp"),
            P("exp", None, "ctx"),
            P("exp", "ctx", None),
        ),
        check_vma=False,
    )
```

```python
import jax
import jax.numpy as jnp
from jax import lax
from jax.experimental import pallas as pl
from jax.experimental.pallas import tpu as pltpu
from jax.sharding import PartitionSpec as P


D = 2048
epsilon = 1e-05
f32 = jnp.float32
bf16 = jnp.bfloat16


def iota(shape, axis):
    return lax.broadcasted_iota(jnp.int32, shape, axis)


def mm(a, b):
    return jnp.dot(a, b, preferred_element_type=f32)


def mm_t(a, b):
    return lax.dot_general(a, b, (((0,), (0,)), ((), ())), preferred_element_type=f32)


def mm_nt(a, b):
    return lax.dot_general(a, b, (((1,), (1,)), ((), ())), preferred_element_type=f32)


def split2(a):
    high = a.astype(bf16)
    return high, (a - high.astype(f32)).astype(bf16)


def split3(a):
    high = a.astype(bf16)
    rest = a - high.astype(f32)
    middle = rest.astype(bf16)
    return high, middle, (rest - middle.astype(f32)).astype(bf16)


def per_head(columns, shape, width):
    lane = iota(shape, 1)
    value = jnp.broadcast_to(columns[:, 0:1], shape)
    for head in range(1, columns.shape[1]):
        value = jnp.where(lane >= head * width, columns[:, head : head + 1], value)
    return value


def ones_where(condition, dtype=bf16):
    return jnp.where(condition, 1.0, 0.0).astype(dtype)


def call(kernel, outs, *args, smem=(), near=(), far=()):
    args = [
        pltpu.with_memory_space_constraint(a, pltpu.VMEM)
        if near is not None and i not in smem and i not in far and a.ndim > 2
        else a
        for i, a in enumerate(args)
    ]
    return pl.pallas_call(
        kernel,
        out_shape=outs,
        in_specs=[
            pl.BlockSpec(memory_space=pltpu.SMEM if i in smem else pltpu.VMEM)
            for i in range(len(args))
        ],
        out_specs=jax.tree.map(lambda o: pl.BlockSpec(memory_space=pltpu.VMEM), outs),
    )(*args)


def shape_of(shape, dtype):
    return jax.ShapeDtypeStruct(shape, dtype)


def route_kernel(ids_ref, ids_t_ref, weight_ref, grad_ref, gain_ref, to_rows_ref, from_ref, pay_ref):
    tokens, features = grad_ref.shape
    experts, _, _ = pay_ref.shape
    rows = to_rows_ref.shape[0]
    capacity = rows // experts
    square = (tokens, tokens)
    grad = grad_ref[...].astype(f32)
    hits_t = [ids_t_ref[k : k + 1, :] == iota(square, 0) for k in range(2)]
    sum_t = ones_where(hits_t[0] | hits_t[1])
    before_t = mm(sum_t, ones_where(iota(square, 0) < iota(square, 1)))
    hits = [ids_ref[:, k : k + 1] == iota(square, 1) for k in range(2)]
    both = ones_where(hits[0] | hits[1])
    before = mm(ones_where(iota(square, 1) < iota(square, 0)), both)
    spread = []
    cot = jnp.zeros((rows, features), f32)
    for k in range(2):
        slot_t = jnp.sum(jnp.where(hits_t[k], before_t, 0.0), axis=0, keepdims=True)
        row_t = ids_t_ref[k : k + 1, :] * capacity + slot_t.astype(jnp.int32)
        table_t = ones_where(iota((rows, tokens), 0) == row_t)
        spread.append(table_t)
        scaled = (weight_ref[:, k : k + 1] * grad).astype(bf16)
        cot = cot + mm(table_t, scaled)
        slot = jnp.sum(jnp.where(hits[k], before, 0.0), axis=1, keepdims=True)
        row = ids_ref[:, k : k + 1] * capacity + slot.astype(jnp.int32)
        from_ref[k] = ones_where(iota((tokens, rows), 1) == row)
    to_rows_ref[...] = spread[0] + spread[1]
    pay_ref[:, :capacity, :] = cot.astype(bf16).reshape(experts, capacity, features)
    high, middle, low = split3(gain_ref[...])
    place = iota((pay_ref.shape[1] - capacity, features), 0)
    pieces = jnp.where(
        place == 0,
        high.astype(f32),
        jnp.where(place == 1, middle.astype(f32), jnp.where(place == 2, low.astype(f32), 0.0)),
    ).astype(bf16)
    pay_ref[:, capacity:, :] = jnp.broadcast_to(pieces[None], (experts,) + pieces.shape)


def state_kernel(x_ref, b_ref, decay_ref, pay_ref, cum_ref):
    tokens, features = x_ref.shape
    heads = decay_ref.shape[0]
    width = features // heads
    square = (tokens, tokens)
    place = iota((features, tokens), 0)
    spread = jnp.broadcast_to(decay_ref[0:1, :], (features, tokens))
    for head in range(1, heads):
        spread = jnp.where(place >= head * width, decay_ref[head : head + 1, :], spread)
    causal = ones_where(iota(square, 0) <= iota(square, 1))
    high, middle, low = split3(spread)
    cum = (mm(high, causal) + mm(middle, causal) + mm(low, causal)).T
    cum_ref[...] = cum
    ending = cum[tokens - 1 : tokens, :]
    tail = jnp.exp(ending - cum)
    moved_high, moved_low = split2(tail * x_ref[...].astype(f32))
    b = b_ref[...]
    state = (mm_t(b, moved_high) + mm_t(b, moved_low)).astype(bf16)
    states = state.shape[0]
    parts = split3(ending)
    place = iota((pay_ref.shape[1] - states, features), 0)
    extra = jnp.where(
        place == 0,
        parts[0].astype(f32),
        jnp.where(place == 1, parts[1].astype(f32), jnp.where(place == 2, parts[2].astype(f32), 0.0)),
    ).astype(bf16)
    for j in range(pay_ref.shape[0]):
        pay_ref[j, :states, :] = state
        pay_ref[j, states:, :] = extra


def local_kernel(x_ref, b_ref, c_ref, cum_ref, skip_ref, residual_ref, local_ref):
    tokens, features = x_ref.shape
    heads = skip_ref.shape[1]
    width = features // heads
    square = (tokens, tokens)
    x = x_ref[...]
    cum = cum_ref[...]
    cum_t = cum.T
    inner = mm_nt(c_ref[...], b_ref[...])
    causal = iota(square, 1) <= iota(square, 0)
    lane = iota((tokens, features), 1)
    skip = per_head(skip_ref[...], (1, features), width)
    total = residual_ref[...].astype(f32) + skip * x.astype(f32)
    for head in range(heads):
        column = cum[:, head * width : head * width + 1]
        row = cum_t[head * width : head * width + 1, :]
        gap = jnp.where(causal, column - row, -jnp.inf)
        high, low = split2(inner * jnp.exp(gap))
        product = mm(high, x) + mm(low, x)
        inside = (lane >= head * width) & (lane < (head + 1) * width)
        total = total + jnp.where(inside, product, 0.0)
    local_ref[...] = total


def back_kernel(b_ref, c_ref, cum_ref, back_ref):
    tokens, features = cum_ref.shape
    heads = back_ref.shape[1]
    width = features // heads
    square = (tokens, tokens)
    cum = cum_ref[...]
    cum_t = cum.T
    inner_t = mm_nt(b_ref[...], c_ref[...])
    causal_t = iota(square, 0) <= iota(square, 1)
    for head in range(heads):
        column = cum[:, head * width : head * width + 1]
        row = cum_t[head * width : head * width + 1, :]
        gap_t = jnp.where(causal_t, row - column, -jnp.inf)
        high, low = split2(inner_t * jnp.exp(gap_t))
        back_ref[0, head] = high
        back_ref[1, head] = low


def block_sums(states_ref, rows_at):
    blocks = states_ref.shape[0]
    features = states_ref.shape[2]
    extra = states_ref[:, rows_at : rows_at + 8, :].astype(f32)
    place = iota((blocks, 8, features), 1)
    return [
        jnp.sum(jnp.where(place == k, extra, 0.0), axis=1).astype(bf16) for k in range(3)
    ]


def weighted(states_ref, weights, states):
    total = jnp.zeros((states, states_ref.shape[2]), f32)
    for j in range(states_ref.shape[0]):
        total = total + weights[j : j + 1, :] * states_ref[j, :states, :].astype(f32)
    return total


def mixed_kernel(me_ref, states_ref, c_ref, cum_ref, local_ref, table_ref, early_ref, mixed_ref, pay_ref, later_ref):
    blocks = states_ref.shape[0]
    states = c_ref.shape[1]
    me = me_ref[0]
    parts = block_sums(states_ref, states)
    source, between = iota((blocks, blocks), 0), iota((blocks, blocks), 1)
    mask = ones_where((between > source) & (between < me))
    sums = mm(mask, parts[0]) + mm(mask, parts[1]) + mm(mask, parts[2])
    which = iota((blocks, states_ref.shape[2]), 0)
    weights = jnp.where(which < me, jnp.exp(sums), 0.0)
    high, low = split2(weighted(states_ref, weights, states))
    c = c_ref[...]
    total = local_ref[...] + jnp.exp(cum_ref[...]) * (mm(c, high) + mm(c, low))
    mixed = total.astype(bf16)
    mixed_ref[...] = mixed
    experts, _, features = pay_ref.shape
    capacity = table_ref.shape[0] // experts
    pay_ref[:, :capacity, :] = (
        mm(table_ref[...], mixed).astype(bf16).reshape(experts, capacity, features)
    )
    pay_ref[:, capacity:, :] = early_ref[...]
    mask = ones_where((between < source) & (between > me))
    sums = mm(mask, parts[0]) + mm(mask, parts[1]) + mm(mask, parts[2])
    later_ref[...] = jnp.where(which > me, jnp.exp(sums), 0.0)


def norm_kernel(in_ref, out_ref, raw_ref, inv_ref, gain_ref):
    peers, _, features = in_ref.shape
    capacity = raw_ref.shape[0]
    square = jnp.zeros((capacity, features), f32)
    for e in range(peers):
        piece = in_ref[e, :capacity, :].astype(f32)
        square = square + piece * piece
    inv = lax.rsqrt(jnp.sum(square, axis=1, keepdims=True) / D + epsilon)
    inv_ref[...] = jnp.broadcast_to(inv, inv_ref.shape)
    for e in range(peers):
        here = slice(e * features, (e + 1) * features)
        piece = in_ref[e, :capacity, :]
        cot = in_ref[e, capacity : 2 * capacity, :]
        gain = jnp.sum(in_ref[e, 2 * capacity :, :].astype(f32), axis=0, keepdims=True)
        gain_ref[:, here] = gain
        raw_ref[:, here] = piece
        normed = (piece.astype(f32) * inv * gain).astype(bf16)
        for j in range(out_ref.shape[0]):
            out_ref[j, :capacity, here] = normed
            out_ref[j, capacity:, here] = cot


def pack_kernel(in_ref, down_ref, out_ref):
    units = down_ref.shape[0]
    for k in range(in_ref.shape[0] // units):
        here = slice(k * units, (k + 1) * units)
        out_ref[0, :, here] = in_ref[here, :]
    out_ref[1] = down_ref[...]


def pack_units(out_ref, lot, activated, d_hidden):
    units = activated.shape[1]
    capacity = out_ref.shape[1] // 2
    for k in range(activated.shape[0] // capacity):
        rows = slice(k * capacity, (k + 1) * capacity)
        here = slice(k * units, (k + 1) * units)
        out_ref[lot, :capacity, here] = activated[rows, :]
        out_ref[lot, capacity:, here] = d_hidden[rows, :]


def expert_kernel(rows_ref, own_ref, peer_ref, near_ref, far_ref, parts_ref, mine_ref, near_units_ref, send_ref, held, sems):
    copies = [
        pltpu.make_async_copy(source, held.at[k], sems.at[k])
        for k, source in enumerate((own_ref, peer_ref, near_ref, far_ref))
    ]
    for copy in copies:
        copy.start()
    chips, both, width = rows_ref.shape
    capacity = both // 2
    count = chips * capacity
    units = held.shape[2]
    blocks = [slice(k * units, (k + 1) * units) for k in range(width // units)]
    rows = rows_ref[:, :capacity, :].reshape(count, width)
    cot = rows_ref[:, capacity:, :].reshape(count, width)
    send_ref[:chips] = rows_ref[...]
    d_total = [None] * len(blocks)
    out_total = None
    for k in range(4):
        copies[k].wait()
        wide = [held[k, 0, :, here] for here in blocks]
        narrow = held[k, 1]
        hidden = mm(rows[:, blocks[0]], wide[0])
        for here, piece in zip(blocks[1:], wide[1:]):
            hidden = hidden + mm(rows[:, here], piece)
        d_act = mm_nt(cot, narrow)
        sigmoid_h = 1.0 / (1.0 + jnp.exp(-hidden))
        activated = (hidden * sigmoid_h).astype(bf16)
        d_hidden = (d_act * sigmoid_h * (1.0 + hidden * (1.0 - sigmoid_h))).astype(bf16)
        if k == 0:
            mine_ref[0] = activated
            mine_ref[1] = d_hidden
        elif k == 2:
            near_units_ref[0] = activated
            near_units_ref[1] = d_hidden
        else:
            pack_units(send_ref, chips + k // 2, activated, d_hidden)
        d_part = [mm_nt(d_hidden, piece) for piece in wide]
        out_part = mm(activated, narrow)
        d_total = d_part if k == 0 else [a + b for a, b in zip(d_total, d_part)]
        out_total = out_part if k == 0 else out_total + out_part
    for here, piece in zip(blocks, d_total):
        parts_ref[:, :capacity, here] = piece.astype(bf16).reshape(chips, capacity, units)
    parts_ref[:, capacity:, :] = out_total.astype(bf16).reshape(chips, capacity, width)


def run_experts(rows, weights):
    chips, both, width = rows.shape
    units = weights[0].shape[1]
    count = chips * both // 2
    near = pl.BlockSpec(memory_space=pltpu.VMEM)
    return pl.pallas_call(
        expert_kernel,
        out_shape=[
            shape_of(rows.shape, bf16),
            shape_of((2, count, units), bf16),
            shape_of((2, count, units), bf16),
            shape_of((chips + 2, both, width), bf16),
        ],
        in_specs=[near] + [pl.BlockSpec(memory_space=pl.ANY)] * 4,
        out_specs=[near] * 4,
        scratch_shapes=[
            pltpu.VMEM((4,) + weights[0].shape, bf16),
            pltpu.SemaphoreType.DMA((4,)),
        ],
    )(pltpu.with_memory_space_constraint(rows, pltpu.VMEM), *weights)


def weight_grad_kernel(own_ref, mine_ref, peer_ref, near_ref, near_units_ref, far_ref, in_ref, down_ref):
    chips, both, width = own_ref.shape
    capacity = both // 2
    count = chips * capacity
    units = mine_ref.shape[2]
    lots = [own_ref, near_ref, peer_ref, far_ref]
    rows = jnp.concatenate([lot[:chips, :capacity, :].reshape(count, width) for lot in lots])
    cot = jnp.concatenate([lot[:chips, capacity:, :].reshape(count, width) for lot in lots])
    activated = [mine_ref[0], near_units_ref[0]]
    d_hidden = [mine_ref[1], near_units_ref[1]]
    for k, lot in enumerate(lots[2:]):
        for j in range(count // capacity):
            here = slice(j * units, (j + 1) * units)
            activated.append(lot[chips + k, :capacity, here])
            d_hidden.append(lot[chips + k, capacity:, here])
    in_ref[...] = mm_t(rows, jnp.concatenate(d_hidden)).astype(bf16)
    down_ref[...] = mm_t(jnp.concatenate(activated), cot).astype(bf16)


def return_kernel(parts_ref, raw_ref, inv_ref, gain_ref, out_ref):
    peers, both, features = out_ref.shape
    capacity = both // 2
    total = parts_ref[0].astype(f32)
    for j in range(1, parts_ref.shape[0]):
        total = total + parts_ref[j].astype(f32)
    d_rows = total[:capacity].astype(bf16).astype(f32)
    out_rows = total[capacity:]
    scaled = gain_ref[...] * d_rows
    raw = raw_ref[...].astype(f32)
    inv = inv_ref[:, 0:1]
    inner = jnp.sum(scaled * raw, axis=1, keepdims=True)
    result = inv * scaled - raw * (inv * inv * inv * inner / D)
    for e in range(peers):
        here = slice(e * features, (e + 1) * features)
        out_ref[e, :capacity, :] = result[:, here].astype(bf16)
        out_ref[e, capacity:, :] = out_rows[:, here].astype(bf16)


def block_out_kernel(rows_ref, from_ref, weight_ref, mixed_ref, out_ref):
    half = rows_ref.shape[1] // 2
    rows = rows_ref[:, half:, :].reshape(from_ref.shape[2], rows_ref.shape[2])
    total = mixed_ref[...].astype(f32)
    extra = weight_ref[:, 0:1] * mm(from_ref[0], rows) + weight_ref[:, 1:2] * mm(from_ref[1], rows)
    out_ref[...] = (total + extra).astype(bf16)


def cot_state_kernel(rows_ref, from_ref, grad_ref, c_ref, cum_ref, residual_ref, wide_ref, pay_ref):
    half = rows_ref.shape[1] // 2
    rows = rows_ref[:, :half, :].reshape(from_ref.shape[2], rows_ref.shape[2])
    table = from_ref[0] + from_ref[1]
    total = grad_ref[...].astype(f32) + mm(table, rows)
    wide_ref[...] = total
    residual_ref[...] = total.astype(bf16)
    high, low = split2(jnp.exp(cum_ref[...]) * total)
    c = c_ref[...]
    state = (mm_t(c, high) + mm_t(c, low)).astype(bf16)
    for j in range(pay_ref.shape[0]):
        pay_ref[j] = state


def back_local_kernel(wide_ref, back_ref, skip_ref, out_ref):
    tokens, features = wide_ref.shape
    heads = back_ref.shape[1]
    width = features // heads
    wide = wide_ref[...]
    high, low = split2(wide)
    lane = iota((tokens, features), 1)
    total = per_head(skip_ref[...], (1, features), width) * wide
    for head in range(heads):
        product = mm(back_ref[0, head], high) + mm(back_ref[1, head], high) + mm(back_ref[0, head], low)
        inside = (lane >= head * width) & (lane < (head + 1) * width)
        total = total + jnp.where(inside, product, 0.0)
    out_ref[...] = total


def final_kernel(states_ref, later_ref, b_ref, cum_ref, local_ref, out_ref):
    tokens = cum_ref.shape[0]
    high, low = split2(weighted(states_ref, later_ref[...], states_ref.shape[1]))
    cum = cum_ref[...]
    tail = jnp.exp(cum[tokens - 1 : tokens, :] - cum)
    b = b_ref[...]
    out_ref[...] = (local_ref[...] + tail * (mm(b, high) + mm(b, low))).astype(bf16)


def swap(a, axis, groups=None):
    return lax.all_to_all(
        a, axis, split_axis=0, concat_axis=0, tiled=True, axis_index_groups=groups
    )


def body(
    residual,
    ssd_input,
    state_in,
    state_out,
    log_decay,
    skip_gain,
    norm_gain,
    route_weight,
    expert_ids,
    weight_in,
    weight_down,
    out_grad,
):
    tokens, features = residual.shape
    heads = log_decay.shape[1]
    states = state_in.shape[1]
    experts = lax.axis_size("exp")
    blocks = lax.axis_size("ctx")
    rows = 2 * tokens
    capacity = rows // experts
    me = lax.axis_index("ctx").astype(jnp.int32).reshape(1)
    skip = skip_gain.reshape(1, heads)
    matrix_in = weight_in[0]
    matrix_down = weight_down[0]

    chips = [(x, y) for x in range(4) for y in range(4)]

    def place(x, y, core):
        return x * 8 + y * 2 + core

    colours = [
        [place(x, y, core) for x, y in chips if (x + y) % 2 == colour]
        for core in range(2)
        for colour in range(2)
    ]
    members = len(colours[0])
    near_of = {}
    for x, y in chips:
        near_of[place(x, y, 0)] = place(x ^ 1, y, 0)
        near_of[place(x, y, 1)] = place(x, y ^ 1, 1)

    def partner(a):
        return lax.ppermute(a, "ctx", [(i, i ^ 1) for i in range(blocks)])

    def near(a):
        return lax.ppermute(a, "ctx", [(i, near_of[i]) for i in range(blocks)])

    state_pay, cum = call(
        state_kernel,
        (shape_of((blocks, states + 8, features), bf16), shape_of((tokens, features), f32)),
        ssd_input, state_in, log_decay.T,
    )
    state_all = swap(state_pay, "ctx")
    own_w = call(
        pack_kernel, shape_of((2,) + matrix_down.shape, bf16), matrix_in, matrix_down
    )
    near_w = near(own_w)
    peer_w = partner(own_w)
    far_w = partner(near_w)

    to_rows, from_rows, cot_pay = call(
        route_kernel,
        (
            shape_of((rows, tokens), bf16),
            shape_of((2, tokens, rows), bf16),
            shape_of((experts, capacity + 8, features), bf16),
        ),
        expert_ids, expert_ids.T, route_weight, out_grad, norm_gain.reshape(1, features),
    )
    local = call(
        local_kernel, shape_of((tokens, features), f32),
        ssd_input, state_in, state_out, cum, skip, residual,
    )
    mixed, rows_pay, later = call(
        mixed_kernel,
        (
            shape_of((tokens, features), bf16),
            shape_of((experts, 2 * capacity + 8, features), bf16),
            shape_of((blocks, features), f32),
        ),
        me, state_all, state_out, cum, local, to_rows, cot_pay,
        smem=(0,),
        far=(6,),
    )
    arrived = swap(rows_pay, "exp")
    spread, raw, inv, gain = call(
        norm_kernel,
        (
            shape_of((members, 2 * capacity, D), bf16),
            shape_of((capacity, D), bf16),
            shape_of((capacity, 128), f32),
            shape_of((1, D), f32),
        ),
        arrived,
    )
    expert_rows = swap(spread, "ctx", colours)

    near_rows = near(expert_rows)
    parts, mine, of_near, send = run_experts(expert_rows, (own_w, peer_w, near_w, far_w))
    parts_all = swap(parts, "ctx", colours)
    peer_lot = partner(send)
    near_units = near(of_near)
    far_lot = near(peer_lot)
    back = call(back_kernel, shape_of((2, heads, tokens, tokens), bf16), state_in, state_out, cum)
    grad_in, grad_down = call(
        weight_grad_kernel,
        (shape_of(matrix_in.shape, bf16), shape_of(matrix_down.shape, bf16)),
        expert_rows, mine, peer_lot, near_rows, near_units, far_lot,
        near=None,
    )

    back_pay = call(
        return_kernel,
        shape_of((experts, 2 * capacity, features), bf16),
        parts_all, raw, inv, gain,
    )
    returned = swap(back_pay, "exp")

    grad_residual, wide, cot_pay_state = call(
        cot_state_kernel,
        (
            shape_of((tokens, features), bf16),
            shape_of((tokens, features), f32),
            shape_of((blocks, states, features), bf16),
        ),
        returned, from_rows, out_grad, state_out, cum,
    )
    cot_states = swap(cot_pay_state, "ctx")
    back_local = call(
        back_local_kernel, shape_of((tokens, features), f32), wide, back, skip
    )
    block_out = call(
        block_out_kernel, shape_of((tokens, features), bf16), returned, from_rows, route_weight, mixed
    )
    grad_input = call(
        final_kernel, shape_of((tokens, features), bf16), cot_states, later, state_in, cum, back_local
    )
    return (block_out, grad_residual, grad_input, grad_in[None], grad_down[None])


def solution(mesh):
    placed = (
        P("ctx", "exp"),
        P("ctx", "exp"),
        P("ctx", None),
        P("ctx", None),
        P("ctx", "exp"),
        P("exp"),
        P("exp"),
        P("ctx", None),
        P("ctx", None),
        P("exp", None, "ctx"),
        P("exp", "ctx", None),
        P("ctx", "exp"),
    )
    return jax.shard_map(
        body,
        mesh=mesh,
        in_specs=placed,
        out_specs=(
            P("ctx", "exp"),
            P("ctx", "exp"),
            P("ctx", "exp"),
            P("exp", None, "ctx"),
            P("exp", "ctx", None),
        ),
        check_vma=False,
    )
```

```python
import jax
import jax.numpy as jnp
from jax import lax
from jax.experimental import pallas as pl
from jax.experimental.pallas import tpu as pltpu
from jax.sharding import PartitionSpec as P


D = 2048
epsilon = 1e-05
f32 = jnp.float32
bf16 = jnp.bfloat16


def iota(shape, axis):
    return lax.broadcasted_iota(jnp.int32, shape, axis)


def mm(a, b):
    return jnp.dot(a, b, preferred_element_type=f32)


def mm_t(a, b):
    return lax.dot_general(a, b, (((0,), (0,)), ((), ())), preferred_element_type=f32)


def mm_nt(a, b):
    return lax.dot_general(a, b, (((1,), (1,)), ((), ())), preferred_element_type=f32)


def split2(a):
    high = a.astype(bf16)
    return high, (a - high.astype(f32)).astype(bf16)


def split3(a):
    high = a.astype(bf16)
    rest = a - high.astype(f32)
    middle = rest.astype(bf16)
    return high, middle, (rest - middle.astype(f32)).astype(bf16)


def per_head(columns, shape, width):
    lane = iota(shape, 1)
    value = jnp.broadcast_to(columns[:, 0:1], shape)
    for head in range(1, columns.shape[1]):
        value = jnp.where(lane >= head * width, columns[:, head : head + 1], value)
    return value


def ones_where(condition, dtype=bf16):
    return jnp.where(condition, 1.0, 0.0).astype(dtype)


def call(kernel, outs, *args, smem=(), near=(), far=()):
    args = [
        pltpu.with_memory_space_constraint(a, pltpu.VMEM)
        if near is not None and i not in smem and i not in far and a.ndim > 2
        else a
        for i, a in enumerate(args)
    ]
    return pl.pallas_call(
        kernel,
        out_shape=outs,
        in_specs=[
            pl.BlockSpec(memory_space=pltpu.SMEM if i in smem else pltpu.VMEM)
            for i in range(len(args))
        ],
        out_specs=jax.tree.map(lambda o: pl.BlockSpec(memory_space=pltpu.VMEM), outs),
    )(*args)


def shape_of(shape, dtype):
    return jax.ShapeDtypeStruct(shape, dtype)


def route_kernel(ids_t_ref, weight_t_ref, grad_ref, gain_ref, to_rows_ref, from_ref, pay_ref, weight_ref):
    tokens, features = grad_ref.shape
    experts, _, _ = pay_ref.shape
    rows = to_rows_ref.shape[0]
    capacity = rows // experts
    square = (tokens, tokens)
    grad = grad_ref[...].astype(f32)
    hits_t = [ids_t_ref[k : k + 1, :] == iota(square, 0) for k in range(2)]
    sum_t = ones_where(hits_t[0] | hits_t[1])
    before_t = mm(sum_t, ones_where(iota(square, 0) < iota(square, 1)))
    ids = [
        jnp.broadcast_to(ids_t_ref[k : k + 1, :].astype(f32), square).T.astype(jnp.int32)
        for k in range(2)
    ]
    hits = [ids[k] == iota(square, 1) for k in range(2)]
    both = ones_where(hits[0] | hits[1])
    before = mm(ones_where(iota(square, 1) < iota(square, 0)), both)
    spread = []
    cot = jnp.zeros((rows, features), f32)
    for k in range(2):
        slot_t = jnp.sum(jnp.where(hits_t[k], before_t, 0.0), axis=0, keepdims=True)
        row_t = ids_t_ref[k : k + 1, :] * capacity + slot_t.astype(jnp.int32)
        table_t = ones_where(iota((rows, tokens), 0) == row_t)
        spread.append(table_t)
        weight = jnp.broadcast_to(weight_t_ref[k : k + 1, :], square).T
        weight_ref[k] = weight
        scaled = (weight * grad).astype(bf16)
        cot = cot + mm(table_t, scaled)
        slot = jnp.sum(jnp.where(hits[k], before, 0.0), axis=1, keepdims=True)
        row = ids[k][:, 0:1] * capacity + slot.astype(jnp.int32)
        from_ref[k] = ones_where(iota((tokens, rows), 1) == row)
    to_rows_ref[...] = spread[0] + spread[1]
    pay_ref[:, :capacity, :] = cot.astype(bf16).reshape(experts, capacity, features)
    high, middle, low = split3(gain_ref[...])
    place = iota((pay_ref.shape[1] - capacity, features), 0)
    pieces = jnp.where(
        place == 0,
        high.astype(f32),
        jnp.where(place == 1, middle.astype(f32), jnp.where(place == 2, low.astype(f32), 0.0)),
    ).astype(bf16)
    pay_ref[:, capacity:, :] = jnp.broadcast_to(pieces[None], (experts,) + pieces.shape)


def state_kernel(x_ref, b_ref, decay_ref, pay_ref, cum_ref):
    tokens, features = x_ref.shape
    heads = decay_ref.shape[0]
    width = features // heads
    square = (tokens, tokens)
    place = iota((features, tokens), 0)
    spread = jnp.broadcast_to(decay_ref[0:1, :], (features, tokens))
    for head in range(1, heads):
        spread = jnp.where(place >= head * width, decay_ref[head : head + 1, :], spread)
    causal = ones_where(iota(square, 0) <= iota(square, 1))
    high, middle, low = split3(spread)
    cum = (mm(high, causal) + mm(middle, causal) + mm(low, causal)).T
    cum_ref[...] = cum
    ending = cum[tokens - 1 : tokens, :]
    tail = jnp.exp(ending - cum)
    moved_high, moved_low = split2(tail * x_ref[...].astype(f32))
    b = b_ref[...]
    state = (mm_t(b, moved_high) + mm_t(b, moved_low)).astype(bf16)
    states = state.shape[0]
    parts = split3(ending)
    place = iota((pay_ref.shape[0] - states, features), 0)
    extra = jnp.where(
        place == 0,
        parts[0].astype(f32),
        jnp.where(place == 1, parts[1].astype(f32), jnp.where(place == 2, parts[2].astype(f32), 0.0)),
    ).astype(bf16)
    pay_ref[:states, :] = state
    pay_ref[states:, :] = extra


def total_of(pay_ref, states):
    return jnp.sum(pay_ref[states:, :].astype(f32), axis=0, keepdims=True)


def chip_state_kernel(me_ref, own_ref, peer_ref, pay_ref):
    first = lax.rem(me_ref[0], 2) == 0
    states = own_ref.shape[0] - 8
    own, peer = total_of(own_ref, states), total_of(peer_ref, states)
    own_scale = jnp.where(first, jnp.exp(peer), 1.0)
    peer_scale = jnp.where(first, 1.0, jnp.exp(own))
    state = (
        own_scale * own_ref[:states, :].astype(f32) + peer_scale * peer_ref[:states, :].astype(f32)
    ).astype(bf16)
    parts = split3(own + peer)
    place = iota((8, state.shape[1]), 0)
    extra = jnp.where(
        place == 0,
        parts[0].astype(f32),
        jnp.where(place == 1, parts[1].astype(f32), jnp.where(place == 2, parts[2].astype(f32), 0.0)),
    ).astype(bf16)
    for j in range(pay_ref.shape[0]):
        pay_ref[j, :states, :] = state
        pay_ref[j, states:, :] = extra


def chip_cot_kernel(me_ref, own_ref, peer_ref, own_pay_ref, peer_pay_ref, pay_ref):
    first = lax.rem(me_ref[0], 2) == 0
    states = own_ref.shape[0]
    own, peer = total_of(own_pay_ref, states), total_of(peer_pay_ref, states)
    own_scale = jnp.where(first, 1.0, jnp.exp(peer))
    peer_scale = jnp.where(first, jnp.exp(own), 1.0)
    state = (own_scale * own_ref[...].astype(f32) + peer_scale * peer_ref[...].astype(f32)).astype(bf16)
    for j in range(pay_ref.shape[0]):
        pay_ref[j] = state


def local_kernel(x_ref, b_ref, c_ref, cum_ref, skip_ref, residual_ref, local_ref):
    tokens, features = x_ref.shape
    heads = skip_ref.shape[1]
    width = features // heads
    square = (tokens, tokens)
    x = x_ref[...]
    cum = cum_ref[...]
    cum_t = cum.T
    inner = mm_nt(c_ref[...], b_ref[...])
    causal = iota(square, 1) <= iota(square, 0)
    lane = iota((tokens, features), 1)
    skip = per_head(skip_ref[...], (1, features), width)
    total = residual_ref[...].astype(f32) + skip * x.astype(f32)
    for head in range(heads):
        column = cum[:, head * width : head * width + 1]
        row = cum_t[head * width : head * width + 1, :]
        gap = jnp.where(causal, column - row, -jnp.inf)
        high, low = split2(inner * jnp.exp(gap))
        product = mm(high, x) + mm(low, x)
        inside = (lane >= head * width) & (lane < (head + 1) * width)
        total = total + jnp.where(inside, product, 0.0)
    local_ref[...] = total


def back_kernel(b_ref, c_ref, cum_ref, back_ref):
    tokens, features = cum_ref.shape
    heads = back_ref.shape[1]
    width = features // heads
    square = (tokens, tokens)
    cum = cum_ref[...]
    cum_t = cum.T
    inner_t = mm_nt(b_ref[...], c_ref[...])
    causal_t = iota(square, 0) <= iota(square, 1)
    for head in range(heads):
        column = cum[:, head * width : head * width + 1]
        row = cum_t[head * width : head * width + 1, :]
        gap_t = jnp.where(causal_t, row - column, -jnp.inf)
        high, low = split2(inner_t * jnp.exp(gap_t))
        back_ref[0, head] = high
        back_ref[1, head] = low


def block_sums(states_ref, rows_at):
    blocks = states_ref.shape[0]
    features = states_ref.shape[2]
    extra = states_ref[:, rows_at : rows_at + 8, :].astype(f32)
    place = iota((blocks, 8, features), 1)
    return [
        jnp.sum(jnp.where(place == k, extra, 0.0), axis=1).astype(bf16) for k in range(3)
    ]


def weighted(states_ref, weights, states):
    total = jnp.zeros((states, states_ref.shape[2]), f32)
    for j in range(states_ref.shape[0]):
        total = total + weights[j : j + 1, :] * states_ref[j, :states, :].astype(f32)
    return total


def mixed_kernel(me_ref, states_ref, peer_ref, c_ref, cum_ref, local_ref, table_ref, early_ref, mixed_ref, pay_ref, later_ref):
    blocks = states_ref.shape[0]
    states = c_ref.shape[1]
    me = lax.div(me_ref[0], 2)
    second = lax.rem(me_ref[0], 2) == 1
    parts = block_sums(states_ref, states)
    source, between = iota((blocks, blocks), 0), iota((blocks, blocks), 1)
    mask = ones_where((between > source) & (between < me))
    sums = mm(mask, parts[0]) + mm(mask, parts[1]) + mm(mask, parts[2])
    which = iota((blocks, states_ref.shape[2]), 0)
    weights = jnp.where(which < me, jnp.exp(sums), 0.0)
    before = weighted(states_ref, weights, states)
    inside = jnp.exp(total_of(peer_ref, states)) * before + peer_ref[:states, :].astype(f32)
    high, low = split2(jnp.where(second, inside, before))
    c = c_ref[...]
    total = local_ref[...] + jnp.exp(cum_ref[...]) * (mm(c, high) + mm(c, low))
    mixed = total.astype(bf16)
    mixed_ref[...] = mixed
    experts, _, features = pay_ref.shape
    capacity = table_ref.shape[0] // experts
    pay_ref[:, :capacity, :] = (
        mm(table_ref[...], mixed).astype(bf16).reshape(experts, capacity, features)
    )
    pay_ref[:, capacity:, :] = early_ref[...]
    mask = ones_where((between < source) & (between > me))
    sums = mm(mask, parts[0]) + mm(mask, parts[1]) + mm(mask, parts[2])
    later_ref[...] = jnp.where(which > me, jnp.exp(sums), 0.0)


def norm_kernel(in_ref, out_ref, raw_ref, inv_ref, gain_ref):
    peers, _, features = in_ref.shape
    capacity = raw_ref.shape[0]
    square = jnp.zeros((capacity, features), f32)
    for e in range(peers):
        piece = in_ref[e, :capacity, :].astype(f32)
        square = square + piece * piece
    inv = lax.rsqrt(jnp.sum(square, axis=1, keepdims=True) / D + epsilon)
    inv_ref[...] = jnp.broadcast_to(inv, inv_ref.shape)
    for e in range(peers):
        here = slice(e * features, (e + 1) * features)
        piece = in_ref[e, :capacity, :]
        cot = in_ref[e, capacity : 2 * capacity, :]
        gain = jnp.sum(in_ref[e, 2 * capacity :, :].astype(f32), axis=0, keepdims=True)
        gain_ref[:, here] = gain
        raw_ref[:, here] = piece
        normed = (piece.astype(f32) * inv * gain).astype(bf16)
        for j in range(out_ref.shape[0]):
            out_ref[j, :capacity, here] = normed
            out_ref[j, capacity:, here] = cot


def pack_kernel(in_ref, down_ref, out_ref):
    units = down_ref.shape[0]
    for k in range(in_ref.shape[0] // units):
        here = slice(k * units, (k + 1) * units)
        out_ref[0, :, here] = in_ref[here, :]
    out_ref[1] = down_ref[...]


def pack_units(out_ref, lot, activated, d_hidden):
    units = activated.shape[1]
    capacity = out_ref.shape[1] // 2
    for k in range(activated.shape[0] // capacity):
        rows = slice(k * capacity, (k + 1) * capacity)
        here = slice(k * units, (k + 1) * units)
        out_ref[lot, :capacity, here] = activated[rows, :]
        out_ref[lot, capacity:, here] = d_hidden[rows, :]


def expert_kernel(
    rows_ref, own_ref, peer_ref, near_ref, far_ref,
    parts_ref, mine_ref, near_units_ref, send_ref,
    wide_ref, narrow_ref, sems,
):
    chips, both, width = rows_ref.shape
    capacity = both // 2
    count = chips * capacity
    units = own_ref.shape[1]
    pieces = width // units
    wide_copies = []
    narrow_copies = []
    for k, source in enumerate((own_ref, peer_ref, near_ref, far_ref)):
        across = pl.ds(k * units, units)
        for j in range(pieces):
            along = pl.ds(j * units, units)
            wide_copies.append(
                pltpu.make_async_copy(
                    source.at[0, :, along], wide_ref.at[along, across], sems.at[k * pieces + j]
                )
            )
        narrow_copies.append(
            pltpu.make_async_copy(source.at[1], narrow_ref.at[across, :], sems.at[4 * pieces + k])
        )
    for copy in wide_copies + narrow_copies:
        copy.start()
    rows = rows_ref[:, :capacity, :].reshape(count, width)
    cot = rows_ref[:, capacity:, :].reshape(count, width)
    send_ref[:chips] = rows_ref[...]
    for copy in wide_copies:
        copy.wait()
    hidden = mm(rows, wide_ref[...])
    sigmoid_h = 1.0 / (1.0 + jnp.exp(-hidden))
    activated = (hidden * sigmoid_h).astype(bf16)
    slope = sigmoid_h * (1.0 + hidden * (1.0 - sigmoid_h))
    for copy in narrow_copies:
        copy.wait()
    d_hidden = (mm_nt(cot, narrow_ref[...]) * slope).astype(bf16)
    parts_ref[:, :capacity, :] = mm_nt(d_hidden, wide_ref[...]).astype(bf16).reshape(chips, capacity, width)
    parts_ref[:, capacity:, :] = mm(activated, narrow_ref[...]).astype(bf16).reshape(chips, capacity, width)
    act = [activated[:, k * units : (k + 1) * units] for k in range(4)]
    d_hid = [d_hidden[:, k * units : (k + 1) * units] for k in range(4)]
    mine_ref[0] = act[0]
    mine_ref[1] = d_hid[0]
    near_units_ref[0] = act[2]
    near_units_ref[1] = d_hid[2]
    pack_units(send_ref, chips, act[1], d_hid[1])
    pack_units(send_ref, chips + 1, act[3], d_hid[3])


def run_experts(rows, weights):
    chips, both, width = rows.shape
    units = weights[0].shape[1]
    count = chips * both // 2
    near = pl.BlockSpec(memory_space=pltpu.VMEM)
    return pl.pallas_call(
        expert_kernel,
        out_shape=[
            shape_of(rows.shape, bf16),
            shape_of((2, count, units), bf16),
            shape_of((2, count, units), bf16),
            shape_of((chips + 2, both, width), bf16),
        ],
        in_specs=[near] + [pl.BlockSpec(memory_space=pl.ANY)] * 4,
        out_specs=[near] * 4,
        scratch_shapes=[
            pltpu.VMEM((width, 4 * units), bf16),
            pltpu.VMEM((4 * units, width), bf16),
            pltpu.SemaphoreType.DMA((4 * (width // units) + 4,)),
        ],
    )(pltpu.with_memory_space_constraint(rows, pltpu.VMEM), *weights)


def weight_grad_kernel(own_ref, mine_ref, peer_ref, near_ref, near_units_ref, far_ref, in_ref, down_ref):
    chips, both, width = own_ref.shape
    capacity = both // 2
    count = chips * capacity
    units = mine_ref.shape[2]
    lots = [own_ref, near_ref, peer_ref, far_ref]
    rows = jnp.concatenate([lot[:chips, :capacity, :].reshape(count, width) for lot in lots])
    cot = jnp.concatenate([lot[:chips, capacity:, :].reshape(count, width) for lot in lots])
    activated = [mine_ref[0], near_units_ref[0]]
    d_hidden = [mine_ref[1], near_units_ref[1]]
    for k, lot in enumerate(lots[2:]):
        for j in range(count // capacity):
            here = slice(j * units, (j + 1) * units)
            activated.append(lot[chips + k, :capacity, here])
            d_hidden.append(lot[chips + k, capacity:, here])
    in_ref[...] = mm_t(rows, jnp.concatenate(d_hidden)).astype(bf16)
    down_ref[...] = mm_t(jnp.concatenate(activated), cot).astype(bf16)


def return_kernel(parts_ref, raw_ref, inv_ref, gain_ref, out_ref):
    peers, both, features = out_ref.shape
    capacity = both // 2
    total = parts_ref[0].astype(f32)
    for j in range(1, parts_ref.shape[0]):
        total = total + parts_ref[j].astype(f32)
    d_rows = total[:capacity].astype(bf16).astype(f32)
    out_rows = total[capacity:]
    scaled = gain_ref[...] * d_rows
    raw = raw_ref[...].astype(f32)
    inv = inv_ref[:, 0:1]
    inner = jnp.sum(scaled * raw, axis=1, keepdims=True)
    result = inv * scaled - raw * (inv * inv * inv * inner / D)
    for e in range(peers):
        here = slice(e * features, (e + 1) * features)
        out_ref[e, :capacity, :] = result[:, here].astype(bf16)
        out_ref[e, capacity:, :] = out_rows[:, here].astype(bf16)


def block_out_kernel(rows_ref, from_ref, weight_ref, mixed_ref, out_ref):
    half = rows_ref.shape[1] // 2
    rows = rows_ref[:, half:, :].reshape(from_ref.shape[2], rows_ref.shape[2])
    total = mixed_ref[...].astype(f32)
    extra = weight_ref[0] * mm(from_ref[0], rows) + weight_ref[1] * mm(from_ref[1], rows)
    out_ref[...] = (total + extra).astype(bf16)


def cot_state_kernel(rows_ref, from_ref, grad_ref, c_ref, cum_ref, residual_ref, wide_ref, state_ref):
    half = rows_ref.shape[1] // 2
    rows = rows_ref[:, :half, :].reshape(from_ref.shape[2], rows_ref.shape[2])
    table = from_ref[0] + from_ref[1]
    total = grad_ref[...].astype(f32) + mm(table, rows)
    wide_ref[...] = total
    residual_ref[...] = total.astype(bf16)
    high, low = split2(jnp.exp(cum_ref[...]) * total)
    c = c_ref[...]
    state_ref[...] = (mm_t(c, high) + mm_t(c, low)).astype(bf16)


def back_local_kernel(wide_ref, back_ref, skip_ref, out_ref):
    tokens, features = wide_ref.shape
    heads = back_ref.shape[1]
    width = features // heads
    wide = wide_ref[...]
    high, low = split2(wide)
    lane = iota((tokens, features), 1)
    total = per_head(skip_ref[...], (1, features), width) * wide
    for head in range(heads):
        product = mm(back_ref[0, head], high) + mm(back_ref[1, head], high) + mm(back_ref[0, head], low)
        inside = (lane >= head * width) & (lane < (head + 1) * width)
        total = total + jnp.where(inside, product, 0.0)
    out_ref[...] = total


def final_kernel(me_ref, states_ref, peer_ref, peer_pay_ref, later_ref, b_ref, cum_ref, local_ref, out_ref):
    tokens = cum_ref.shape[0]
    states = states_ref.shape[1]
    after = weighted(states_ref, later_ref[...], states)
    inside = jnp.exp(total_of(peer_pay_ref, states)) * after + peer_ref[...].astype(f32)
    high, low = split2(jnp.where(lax.rem(me_ref[0], 2) == 0, inside, after))
    cum = cum_ref[...]
    tail = jnp.exp(cum[tokens - 1 : tokens, :] - cum)
    b = b_ref[...]
    out_ref[...] = (local_ref[...] + tail * (mm(b, high) + mm(b, low))).astype(bf16)


def swap(a, axis, groups=None):
    return lax.all_to_all(
        a, axis, split_axis=0, concat_axis=0, tiled=True, axis_index_groups=groups
    )


def body(
    residual,
    ssd_input,
    state_in,
    state_out,
    log_decay,
    skip_gain,
    norm_gain,
    route_weight,
    expert_ids,
    weight_in,
    weight_down,
    out_grad,
):
    tokens, features = residual.shape
    heads = log_decay.shape[1]
    states = state_in.shape[1]
    experts = lax.axis_size("exp")
    blocks = lax.axis_size("ctx")
    rows = 2 * tokens
    capacity = rows // experts
    me = lax.axis_index("ctx").astype(jnp.int32).reshape(1)
    skip = skip_gain.reshape(1, heads)
    matrix_in = weight_in[0]
    matrix_down = weight_down[0]

    chips = [(x, y) for x in range(4) for y in range(4)]

    def place(x, y, core):
        return x * 8 + y * 2 + core

    colours = [
        [place(x, y, core) for x, y in chips if (x + y) % 2 == colour]
        for core in range(2)
        for colour in range(2)
    ]
    members = len(colours[0])
    same_core = [[place(x, y, core) for x, y in chips] for core in range(2)]
    near_of = {}
    for x, y in chips:
        near_of[place(x, y, 0)] = place(x ^ 1, y, 0)
        near_of[place(x, y, 1)] = place(x, y ^ 1, 1)

    def partner(a):
        return lax.ppermute(a, "ctx", [(i, i ^ 1) for i in range(blocks)])

    def near(a):
        return lax.ppermute(a, "ctx", [(i, near_of[i]) for i in range(blocks)])

    state_pay, cum = call(
        state_kernel,
        (shape_of((states + 8, features), bf16), shape_of((tokens, features), f32)),
        ssd_input, state_in, log_decay.T,
    )
    peer_pay = partner(state_pay)
    chip_pay = call(
        chip_state_kernel,
        shape_of((blocks // 2, states + 8, features), bf16),
        me, state_pay, peer_pay,
        smem=(0,),
    )
    state_all = swap(chip_pay, "ctx", same_core)
    own_w = call(
        pack_kernel, shape_of((2,) + matrix_down.shape, bf16), matrix_in, matrix_down
    )
    near_w = near(own_w)
    peer_w = partner(own_w)
    far_w = partner(near_w)

    to_rows, from_rows, cot_pay, weight_wide = call(
        route_kernel,
        (
            shape_of((rows, tokens), bf16),
            shape_of((2, tokens, rows), bf16),
            shape_of((experts, capacity + 8, features), bf16),
            shape_of((2, tokens, features), f32),
        ),
        expert_ids.T, route_weight.T, out_grad, norm_gain.reshape(1, features),
    )
    local = call(
        local_kernel, shape_of((tokens, features), f32),
        ssd_input, state_in, state_out, cum, skip, residual,
    )
    mixed, rows_pay, later = call(
        mixed_kernel,
        (
            shape_of((tokens, features), bf16),
            shape_of((experts, 2 * capacity + 8, features), bf16),
            shape_of((blocks // 2, features), f32),
        ),
        me, state_all, peer_pay, state_out, cum, local, to_rows, cot_pay,
        smem=(0,),
        far=(7,),
    )
    arrived = swap(rows_pay, "exp")
    spread, raw, inv, gain = call(
        norm_kernel,
        (
            shape_of((members, 2 * capacity, D), bf16),
            shape_of((capacity, D), bf16),
            shape_of((capacity, 128), f32),
            shape_of((1, D), f32),
        ),
        arrived,
    )
    expert_rows = swap(spread, "ctx", colours)

    near_rows = near(expert_rows)
    parts, mine, of_near, send = run_experts(expert_rows, (own_w, peer_w, near_w, far_w))
    parts_all = swap(parts, "ctx", colours)
    peer_lot = partner(send)
    near_units = near(of_near)
    far_lot = near(peer_lot)
    back = call(
        back_kernel, shape_of((2, heads, tokens, tokens), bf16), state_in, state_out, cum
    )
    grad_in, grad_down = call(
        weight_grad_kernel,
        (shape_of(matrix_in.shape, bf16), shape_of(matrix_down.shape, bf16)),
        expert_rows, mine, peer_lot, near_rows, near_units, far_lot,
        near=None,
    )

    back_pay = call(
        return_kernel,
        shape_of((experts, 2 * capacity, features), bf16),
        parts_all, raw, inv, gain,
    )
    returned = swap(back_pay, "exp")

    grad_residual, wide, cot_state = call(
        cot_state_kernel,
        (
            shape_of((tokens, features), bf16),
            shape_of((tokens, features), f32),
            shape_of((states, features), bf16),
        ),
        returned, from_rows, out_grad, state_out, cum,
    )
    peer_cot = partner(cot_state)
    cot_chip = call(
        chip_cot_kernel,
        shape_of((blocks // 2, states, features), bf16),
        me, cot_state, peer_cot, state_pay, peer_pay,
        smem=(0,),
    )
    cot_states = swap(cot_chip, "ctx", same_core)
    back_local = call(
        back_local_kernel, shape_of((tokens, features), f32), wide, back, skip
    )
    block_out = call(
        block_out_kernel, shape_of((tokens, features), bf16), returned, from_rows, weight_wide, mixed
    )
    grad_input = call(
        final_kernel, shape_of((tokens, features), bf16), me, cot_states, peer_cot, peer_pay, later, state_in, cum, back_local,
        smem=(0,),
    )
    return (block_out, grad_residual, grad_input, grad_in[None], grad_down[None])


def solution(mesh):
    placed = (
        P("ctx", "exp"),
        P("ctx", "exp"),
        P("ctx", None),
        P("ctx", None),
        P("ctx", "exp"),
        P("exp"),
        P("exp"),
        P("ctx", None),
        P("ctx", None),
        P("exp", None, "ctx"),
        P("exp", "ctx", None),
        P("ctx", "exp"),
    )
    return jax.shard_map(
        body,
        mesh=mesh,
        in_specs=placed,
        out_specs=(
            P("ctx", "exp"),
            P("ctx", "exp"),
            P("ctx", "exp"),
            P("exp", None, "ctx"),
            P("exp", "ctx", None),
        ),
        check_vma=False,
    )
```
